32 devices in a mesh: dp: 8 (over z, y), seq: 4 (over x, core).
Axes of the slice: x: 2, y: 2, z: 4, core: 2. Of those that a mesh axis runs over, the one named last changes fastest.
Arguments:
- inputs: bfloat16 [8, 1024, 768], P('dp', 'seq'), may hold values from -6 to 6
- lengths: int32 [8], P('dp'), may hold values from 1 to 1024, 6144 in all
- gain_attend: bfloat16 [2, 768], P(None, ('dp', 'seq')), may hold values from 0.5 to 1.5
- shift_attend: bfloat16 [2, 768], P(None, ('dp', 'seq')), may hold values from -1.5 to 1.5
- weight_query: bfloat16 [2, 768, 768], P(None, ('dp', 'seq')), may hold values from -0.3125 to 0.3125
- weight_key: bfloat16 [2, 768, 768], P(None, ('dp', 'seq')), may hold values from -0.3125 to 0.3125
- weight_value: bfloat16 [2, 768, 768], P(None, ('dp', 'seq')), may hold values from -0.21875 to 0.21875
- weight_output: bfloat16 [2, 768, 768], P(None, ('dp', 'seq')), may hold values from -0.875 to 0.875
- gain_mixer: bfloat16 [2, 768], P(None, ('dp', 'seq')), may hold values from 0.5 to 1.5
- shift_mixer: bfloat16 [2, 768], P(None, ('dp', 'seq')), may hold values from -1.5 to 1.5
- weight_inner: bfloat16 [2, 768, 3072], P(None, ('dp', 'seq')), may hold values from -0.21875 to 0.21875
- bias_inner: bfloat16 [2, 3072], P(None, ('dp', 'seq')), may hold values from -2.5 to 2.5
- weight_outer: bfloat16 [2, 3072, 768], P(None, ('dp', 'seq')), may hold values from -0.109375 to 0.109375
- bias_outer: bfloat16 [2, 768], P(None, ('dp', 'seq')), may hold values from -1.5 to 1.5
- cotangent: float32 [8, 1024, 768], P('dp', 'seq'), may hold values from -6 to 6
Outputs:
- output: float32 [8, 1024, 768], P('dp', 'seq')
- input_grad: float32 [8, 1024, 768], P('dp', 'seq')
- grad_gain_attend: float32 [2, 768], P(None, ('dp', 'seq'))
- grad_shift_attend: float32 [2, 768], P(None, ('dp', 'seq'))
- grad_weight_query: float32 [2, 768, 768], P(None, ('dp', 'seq'))
- grad_weight_key: float32 [2, 768, 768], P(None, ('dp', 'seq'))
- grad_weight_value: float32 [2, 768, 768], P(None, ('dp', 'seq'))
- grad_weight_output: float32 [2, 768, 768], P(None, ('dp', 'seq'))
- grad_gain_mixer: float32 [2, 768], P(None, ('dp', 'seq'))
- grad_shift_mixer: float32 [2, 768], P(None, ('dp', 'seq'))
- grad_weight_inner: float32 [2, 768, 3072], P(None, ('dp', 'seq'))
- grad_bias_inner: float32 [2, 3072], P(None, ('dp', 'seq'))
- grad_weight_outer: float32 [2, 3072, 768], P(None, ('dp', 'seq'))
- grad_bias_outer: float32 [2, 768], P(None, ('dp', 'seq'))
- selected_share: float32 [], replicated
The draws below stay inside these ranges and needn't reach their ends.
Inputs may be any that keep to these rules, and one draw needn't show every extreme that they name: `lengths`: each sequence's count of real tokens; the longest sequence has exactly 1024.
All inputs are finite; a program needn't handle non-finite values. No bound on the sum of `lengths` on one device may be relied on, other than what follows from the above.
Results may differ from the reference program's by a relative error of at most 0.024.
Values may be sent and summed in bfloat16 or wider, within the bound.
No kernel may reach another device: no remote copies, remote signals or barrier semaphores. Data moves between devices by JAX's collectives and lax.ppermute only.
A program may use at most 320 MiB of HBM per device.

```python
import math
import jax
import jax.numpy as jnp
import numpy as np
from jax import lax

D = 768
HEADS = 12
FF = 3072
HEAD = 64
LEN = 1024
LAYERS = 2
SEQS = 8


def block_scale(rng, shape, shards, least, top_value):
    factor_of = 1.0
    for dim, blocks in shards:
        heights = jax.random.uniform(jax.random.fold_in(jax.random.fold_in(rng, 6), dim), (blocks,), jnp.float32, least / len(shards), top_value / len(shards))
        factor_of = factor_of * jnp.repeat(jnp.exp(heights), shape[dim] // blocks).reshape((-1,) + (1,) * (len(shape) - 1 - dim))
    return factor_of


def profile(amount, total, bound, lean):
    loads = [(1 << 20) // math.isqrt(grade ** lean) + 1 for grade in range(2, amount + 1)]
    surplus, holding = total - bound - (amount - 1), [1] * (amount - 1)
    while surplus > 0:
        free = [i for i in range(amount - 1) if holding[i] < bound]
        whole, remaining = sum([loads[i] for i in free]), surplus
        for i in free:
            more = min(bound - holding[i], max(1, remaining * loads[i] // whole), surplus)
            holding[i] = holding[i] + more
            surplus = surplus - more
    return np.array([bound] + holding)


def ragged(key, count, total, limit, lean):
    if count == 2:
        one = jax.random.randint(key, (), max(1, total - limit), min(limit, total - 1) + 1)
        return jnp.stack([one, total - one])
    sizes = jnp.asarray(profile(count, total, limit, lean), jnp.int32)
    couples = (count - 1) // 2
    donor, taker = sizes[1:1 + 2 * couples:2], sizes[2:2 + 2 * couples:2]
    room = jnp.minimum(donor - 1, limit - taker)
    shifted = jax.random.randint(jax.random.fold_in(key, 1), (couples,), 0, 1 << 20) % (room + 1)
    sizes = sizes.at[1:1 + 2 * couples:2].set(donor - shifted).at[2:2 + 2 * couples:2].set(taker + shifted)
    return sizes[jax.random.permutation(jax.random.fold_in(key, 2), count)]


def gaussian(stream_key, dims, deviation, limit, shards=(), kind=jnp.bfloat16):
    array = jax.random.normal(stream_key, dims, jnp.float32) * deviation
    if len(shards) > 0:
        array = block_scale(stream_key, dims, shards, -0.22, 0.18) * array
    return jnp.clip(array, min=-limit, max=limit).astype(kind)


def setup_inputs(seed: int = 0) -> dict:
    streams_of = jax.random.split(jax.random.key(seed), 16)
    inputs = gaussian(streams_of[0], (SEQS, LEN, D), 1.0, 6.0, ((0, 8), (1, 4)))
    lengths = ragged(streams_of[1], SEQS, SEQS * LEN * 3 // 4, LEN, 2).astype(jnp.int32)
    gain_attend = jnp.clip(1.0 + 0.1 * jax.random.normal(streams_of[2], (LAYERS, D), jnp.float32), 0.5, 1.5).astype(jnp.bfloat16)
    shift_attend = gaussian(streams_of[3], (LAYERS, D), 0.3, 1.5, ((1, 32),))
    weight_query = gaussian(streams_of[4], (LAYERS, D, D), (D // 2) ** -0.5, 0.3125, ((1, 32),))
    weight_key = gaussian(streams_of[5], (LAYERS, D, D), (D // 2) ** -0.5, 0.3125, ((1, 32),))
    weight_value = gaussian(streams_of[6], (LAYERS, D, D), D ** -0.5, 0.21875, ((1, 32),))
    weight_output = gaussian(streams_of[7], (LAYERS, D, D), (D // 16) ** -0.5, 0.875, ((1, 32),))
    gain_mixer = jnp.clip(1.0 + 0.1 * jax.random.normal(streams_of[8], (LAYERS, D), jnp.float32), 0.5, 1.5).astype(jnp.bfloat16)
    shift_mixer = gaussian(streams_of[9], (LAYERS, D), 0.3, 1.5, ((1, 32),))
    weight_inner = gaussian(streams_of[10], (LAYERS, D, FF), D ** -0.5, 0.21875, ((1, 32),))
    bias_inner = gaussian(streams_of[11], (LAYERS, FF), 0.5, 2.5, ((1, 32),))
    weight_outer = gaussian(streams_of[12], (LAYERS, FF, D), FF ** -0.5, 0.109375, ((1, 32),))
    bias_outer = gaussian(streams_of[13], (LAYERS, D), 0.3, 1.5, ((1, 32),))
    cotangent = gaussian(streams_of[14], (SEQS, LEN, D), 1.0, 6.0, ((0, 8), (1, 4)), jnp.float32)
    return {"inputs": inputs, "lengths": lengths, "gain_attend": gain_attend, "shift_attend": shift_attend, "weight_query": weight_query, "weight_key": weight_key, "weight_value": weight_value, "weight_output": weight_output, "gain_mixer": gain_mixer, "shift_mixer": shift_mixer, "weight_inner": weight_inner, "bias_inner": bias_inner, "weight_outer": weight_outer, "bias_outer": bias_outer, "cotangent": cotangent}


@jax.custom_vjp
def low(v):
    return lax.optimization_barrier(v.astype(jnp.bfloat16)).astype(jnp.float32)

@jax.custom_vjp
def low_back(v):
    return v

def low_keep(v):
    return (low(v), None)

def low_pass(kept, grad):
    return (grad,)

def back_keep(v):
    return (v, None)

def back_low(kept, grad):
    return (low(grad),)
low.defvjp(low_keep, low_pass)
low_back.defvjp(back_keep, back_low)
norm_eps = 1e-05
share_level = 0.5
select_strength = 2.0
masked_value = -1e+30

def hdot(left, right):
    return jnp.dot(left, right, precision=lax.Precision.HIGHEST, preferred_element_type=jnp.float32)

def layer_norm(hidden, gain, shift):
    average = lax.optimization_barrier(jnp.mean(hidden, axis=-1, keepdims=True))
    centered = hidden - average
    spread = lax.optimization_barrier(jnp.mean(centered * centered, axis=-1, keepdims=True))
    return centered * lax.rsqrt(spread + norm_eps) * gain + shift

def block_layer(hidden, lens_group, params):
    gain_a, shift_a, w_query, w_key, w_value, w_output, gain_m, shift_m, w_inner, b_inner, w_outer, b_outer = params
    groups = hidden.shape[0]
    highest = lax.Precision.HIGHEST
    normed = low(layer_norm(hidden, gain_a, shift_a)).reshape(groups * LEN, D)
    query = low_back(low(hdot(normed, w_query))).reshape(groups, LEN, HEADS, HEAD)
    keys = low_back(low(hdot(normed, w_key))).reshape(groups, LEN, HEADS, HEAD)
    values = low_back(low(hdot(normed, w_value))).reshape(groups, LEN, HEADS, HEAD)
    scores = low_back(jnp.einsum('gqhe,gkhe->ghqk', query, keys, precision=highest) * 0.125)
    place = jnp.arange(LEN, dtype=jnp.int32)
    valid = place[None, :] < lens_group[:, None]
    pick = (place[None, :, None] > place[None, None, :]) & (place[None, None, :] >= 1) & valid[:, :, None] & valid[:, None, :]
    select = jnp.where(pick, jax.nn.relu(scores[:, 0]), 0.0) * (select_strength / LEN)
    inclusive = jnp.cumsum(select, axis=1)
    carried = inclusive - select
    allowed = (place[None, :, None] >= place[None, None, :]) & valid[:, None, :]
    logits = jnp.where(allowed[:, None], scores - carried[:, None], masked_value)
    probs = low(jax.nn.softmax(logits, axis=-1))
    mixed = low_back(low(jnp.einsum('ghqk,gkhe->gqhe', probs, values, precision=highest))).reshape(groups * LEN, D)
    after = hidden + low_back(hdot(mixed, w_output)).reshape(groups, LEN, D)
    normed_two = low(layer_norm(after, gain_m, shift_m)).reshape(groups * LEN, D)
    inner = low_back(hdot(normed_two, w_inner) + b_inner)
    active = low(jax.nn.gelu(inner))
    outer = low_back(hdot(active, w_outer) + b_outer)
    result = after + outer.reshape(groups, LEN, D)
    totals = inclusive[:, -1, :]
    share = jnp.sum(jnp.where(valid, jnp.minimum(totals / share_level, 1.0), 0.0))
    return (result, share)

def reference(inputs, lengths, gain_attend, shift_attend, weight_query, weight_key, weight_value, weight_output, gain_mixer, shift_mixer, weight_inner, bias_inner, weight_outer, bias_outer, cotangent):
    weights = (gain_attend, shift_attend, weight_query, weight_key, weight_value, weight_output, gain_mixer, shift_mixer, weight_inner, bias_inner, weight_outer, bias_outer)
    floats = tuple((piece.astype(jnp.float32) for piece in weights))
    group = 4 if SEQS % 4 == 0 else 2 if SEQS % 2 == 0 else 1
    blocks = SEQS // group
    grouped_lengths = lengths.reshape(blocks, group)

    def forward(hidden_all, params_all):

        def step(carry, item):
            hidden, lens_group = item
            share = jnp.zeros((), jnp.float32)
            for layer_index in range(LAYERS):
                params = tuple((piece[layer_index] for piece in params_all))
                hidden, part = block_layer(hidden, lens_group, params)
                share = share + part
            return (carry + share, hidden)
        share_total, outputs = lax.scan(jax.checkpoint(step), jnp.zeros((), jnp.float32), (hidden_all.reshape(blocks, group, LEN, D), grouped_lengths))
        return (outputs.reshape(SEQS, LEN, D), share_total)
    result, pullback, share_total = jax.vjp(forward, inputs.astype(jnp.float32), floats, has_aux=True)
    input_grad, grads = pullback(cotangent.astype(jnp.float32))
    selected = share_total / (LAYERS * jnp.sum(lengths).astype(jnp.float32))
    return (result, input_grad, grads[0], grads[1], grads[2], grads[3], grads[4], grads[5], grads[6], grads[7], grads[8], grads[9], grads[10], grads[11], selected)
```

```python
import jax
import jax.numpy as jnp
from jax import lax
from jax.sharding import PartitionSpec as P

HEADS = 12


norm_eps = 1e-05
share_level = 0.5
select_strength = 2.0
masked_value = -1e30


def layer_norm(hidden, gain, shift):
    average = jnp.mean(hidden, axis=-1, keepdims=True)
    centered = hidden - average
    spread = jnp.mean(centered * centered, axis=-1, keepdims=True)
    return centered * lax.rsqrt(spread + norm_eps) * gain + shift


def product(left, right, form):
    return jnp.einsum(form, left, right, preferred_element_type=jnp.float32)


def flip(array, axis, bit):
    size = lax.axis_size(axis)
    return lax.ppermute(array, axis, [(i, i ^ bit) for i in range(size)])


def bits_of(axis):
    size = lax.axis_size(axis)
    return [1 << k for k in range(size.bit_length() - 1)]


def upper(axis, bit):
    return (lax.axis_index(axis) & bit) != 0


def gather_line(array, axis):
    blocks = array[None]
    for bit in reversed(bits_of(axis)):
        other = flip(blocks, axis, bit)
        is_upper = upper(axis, bit)
        low = jnp.where(is_upper, other, blocks)
        high = jnp.where(is_upper, blocks, other)
        blocks = jnp.stack([low, high])
        blocks = blocks.reshape((-1,) + array.shape)
    steps = len(bits_of(axis))
    blocks = blocks.reshape((2,) * steps + array.shape)
    order = tuple(reversed(range(steps))) + tuple(range(steps, blocks.ndim))
    return blocks.transpose(order).reshape((-1,) + array.shape)


def scatter_line(blocks, axis):
    steps = len(bits_of(axis))
    rest = blocks.shape[1:]
    blocks = blocks.reshape((2,) * steps + rest)
    for bit in bits_of(axis):
        is_upper = upper(axis, bit)
        low = lax.index_in_dim(blocks, 0, blocks.ndim - len(rest) - 1, False)
        high = lax.index_in_dim(blocks, 1, blocks.ndim - len(rest) - 1, False)
        keep = jnp.where(is_upper, high, low)
        send = jnp.where(is_upper, low, high)
        blocks = keep + flip(send, axis, bit)
    return blocks


def line_prefix(array, axis, reverse):
    total = array
    before = jnp.zeros_like(array)
    for bit in bits_of(axis):
        other = flip(total, axis, bit)
        is_upper = upper(axis, bit)
        take = jnp.logical_not(is_upper) if reverse else is_upper
        before = before + jnp.where(take, other, 0.0)
        total = total + other
    return before, total


def sum_all(array, axes):
    for axis in axes:
        for bit in bits_of(axis):
            array = array + flip(array, axis, bit)
    return array


def pack_weights(w_query, w_key, w_value, w_output, w_inner, w_outer):
    rows, width = w_query.shape
    parts = w_inner.shape[1] // width
    inner = w_inner.reshape(rows, parts, width).transpose(1, 0, 2)
    outer = w_outer.reshape(parts, rows, width)
    square = jnp.stack([w_query, w_key, w_value, w_output])
    return jnp.concatenate([square, inner, outer])


def unpack_outer(planes, devices):
    parts, rows, width = planes.shape
    split = planes.reshape(parts, devices, rows // devices, width)
    return split.transpose(1, 0, 2, 3).reshape(parts * rows, width)


def pack_outer(grad, parts, devices):
    rows, width = grad.shape
    split = grad.reshape(devices, parts, rows // (parts * devices), width)
    return split.transpose(1, 0, 2, 3).reshape(parts, rows // parts, width)


def local(
    inputs,
    lengths,
    gain_attend,
    shift_attend,
    weight_query,
    weight_key,
    weight_value,
    weight_output,
    gain_mixer,
    shift_mixer,
    weight_inner,
    bias_inner,
    weight_outer,
    bias_outer,
    cotangent,
):
    layers = gain_attend.shape[0]
    seq_dev, local_len, width = inputs.shape
    heads = HEADS
    head = width // heads
    seq_count = lax.axis_size("seq")
    devices = lax.axis_size(("dp", "seq"))
    full_len = local_len * seq_count
    highest = lax.Precision.HIGHEST
    is_last = lax.axis_index("seq") == seq_count - 1
    position = lax.axis_index("seq") * local_len + jnp.arange(local_len, dtype=jnp.int32)
    key_place = jnp.arange(full_len, dtype=jnp.int32)
    valid_keys = key_place[None, :] < lengths[:, None]
    valid_query = position[None, :] < lengths[:, None]
    select_mask = (
        (position[None, :, None] > key_place[None, None, :])
        & (key_place[None, None, :] >= 1)
        & valid_query[:, :, None]
        & valid_keys[:, None, :]
    )
    allowed = ((position[None, :, None] >= key_place[None, None, :]) & valid_keys[:, None, :])[
        :, None
    ]
    row_index = jnp.arange(local_len, dtype=jnp.int32)
    strict_lower = (row_index[:, None] > row_index[None, :]).astype(jnp.float32)
    select_scale = select_strength / full_len

    both = ("dp", "seq")
    parts = weight_inner.shape[2] // width
    vectors = jnp.concatenate(
        [gain_attend, shift_attend, gain_mixer, shift_mixer, bias_outer, bias_inner], axis=1
    )
    vector_rows = gather_line(gather_line(vectors, "seq"), "dp")
    per = width // devices
    vector_rows = vector_rows.reshape(devices, layers, -1)
    small = [
        vector_rows[:, :, k * per : (k + 1) * per].transpose(1, 0, 2).reshape(layers, width)
        for k in range(5)
    ]
    small.append(
        vector_rows[:, :, 5 * per :].transpose(1, 0, 2).reshape(layers, parts * width)
    )
    whole = [
        lax.all_gather(
            pack_weights(
                weight_query[k],
                weight_key[k],
                weight_value[k],
                weight_output[k],
                weight_inner[k],
                weight_outer[k],
            ),
            both,
            axis=1,
            tiled=True,
        )
        for k in range(layers)
    ]
    w_outers = [unpack_outer(planes[4 + parts :], devices) for planes in whole]

    def score_block(query, keys_whole):
        scores = (
            product(query, keys_whole.reshape(seq_dev, full_len, heads, head), "sqhe,skhe->shqk")
            * 0.125
        )
        select = jnp.where(select_mask, jax.nn.relu(scores[:, 0]), 0.0) * select_scale
        return (scores, select)

    def logits_from(scores, select, before):
        carried = before[:, None, :] + jnp.einsum(
            "qr,srk->sqk", strict_lower, select, precision=highest
        )
        return jnp.where(allowed, scores - carried[:, None], masked_value)

    hidden = inputs.astype(jnp.float32)
    share_sum = jnp.zeros((), jnp.float32)
    saved = []
    for layer_index in range(layers):
        planes = whole[layer_index]
        forward_gain_a, forward_shift_a, forward_gain_m, forward_shift_m = (
            small[k][layer_index] for k in range(4)
        )
        forward_b_outer, forward_b_inner = (small[k][layer_index] for k in (4, 5))
        forward_w_query, forward_w_key, forward_w_value, forward_w_output = (
            planes[k] for k in range(4)
        )
        forward_w_inner = planes[4 : 4 + parts].transpose(1, 0, 2).reshape(width, parts * width)
        forward_w_outer = w_outers[layer_index]
        forward_normed = (
            layer_norm(
                hidden, forward_gain_a.astype(jnp.float32), forward_shift_a.astype(jnp.float32)
            )
            .astype(jnp.bfloat16)
            .reshape(-1, width)
        )
        forward_query = (
            jnp.dot(forward_normed, forward_w_query, preferred_element_type=jnp.float32)
            .astype(jnp.bfloat16)
            .reshape(seq_dev, local_len, heads, head)
        )
        forward_keys = (
            jnp.dot(forward_normed, forward_w_key, preferred_element_type=jnp.float32)
            .astype(jnp.bfloat16)
            .reshape(seq_dev, local_len, width)
        )
        forward_values = (
            jnp.dot(forward_normed, forward_w_value, preferred_element_type=jnp.float32)
            .astype(jnp.bfloat16)
            .reshape(seq_dev, local_len, width)
        )
        forward_keys_whole = (
            gather_line(forward_keys, "seq").transpose(1, 0, 2, 3).reshape(seq_dev, full_len, width)
        )
        forward_values_whole = (
            gather_line(forward_values, "seq")
            .transpose(1, 0, 2, 3)
            .reshape(seq_dev, full_len, width)
        )
        forward_scores, forward_select = score_block(forward_query, forward_keys_whole)
        column = jnp.sum(forward_select, axis=1)
        forward_before, totals = line_prefix(column, "seq", False)
        logits = logits_from(forward_scores, forward_select, forward_before)
        peak = jnp.max(logits, axis=-1, keepdims=True)
        expo = jnp.exp(logits - peak)
        denominator = jnp.sum(expo, axis=-1, keepdims=True)
        forward_probs = expo / denominator
        forward_log_total = peak + jnp.log(denominator)
        forward_mixed = (
            product(
                forward_probs.astype(jnp.bfloat16),
                forward_values_whole.reshape(seq_dev, full_len, heads, head),
                "shqk,skhe->sqhe",
            )
            .astype(jnp.bfloat16)
            .reshape(-1, width)
        )
        forward_after = hidden + jnp.dot(
            forward_mixed, forward_w_output, preferred_element_type=jnp.float32
        ).reshape(hidden.shape)
        forward_normed_two = (
            layer_norm(
                forward_after,
                forward_gain_m.astype(jnp.float32),
                forward_shift_m.astype(jnp.float32),
            )
            .astype(jnp.bfloat16)
            .reshape(-1, width)
        )
        forward_inner = jnp.dot(
            forward_normed_two, forward_w_inner, preferred_element_type=jnp.float32
        ) + forward_b_inner.astype(jnp.float32)
        forward_active = jax.nn.gelu(forward_inner).astype(jnp.bfloat16)
        outer = jnp.dot(
            forward_active, forward_w_outer, preferred_element_type=jnp.float32
        ) + forward_b_outer.astype(jnp.float32)
        result = forward_after + outer.reshape(hidden.shape)
        share = jnp.where(
            is_last,
            jnp.sum(jnp.where(valid_keys, jnp.minimum(totals / share_level, 1.0), 0.0)),
            0.0,
        )
        forward_kept = (
            hidden,
            forward_normed,
            forward_query,
            forward_keys,
            forward_values,
            forward_keys_whole,
            forward_values_whole,
            forward_before,
            forward_log_total,
            forward_mixed,
            forward_after,
            forward_normed_two,
            forward_inner,
            forward_active,
        )
        hidden = result
        share_sum = share_sum + share
        saved.append(forward_kept)
    grad_hidden = cotangent
    reduced = [None] * layers
    vector_grads = [None] * layers
    for layer_index in reversed(range(layers)):
        planes = whole[layer_index]
        gain_a, shift_a, gain_m, shift_m = (small[k][layer_index] for k in range(4))
        w_query, w_key, w_value, w_output = (planes[k] for k in range(4))
        w_inner = planes[4 : 4 + parts].transpose(1, 0, 2).reshape(width, parts * width)
        w_outer = w_outers[layer_index]
        (
            backward_hidden,
            normed,
            backward_query,
            keys,
            values,
            backward_keys_whole,
            values_whole,
            backward_before,
            log_total,
            mixed,
            after,
            normed_two,
            inner,
            active,
        ) = saved[layer_index]
        grad_y = grad_hidden.astype(jnp.bfloat16).reshape(-1, width)
        grad_b_outer = jnp.sum(grad_y, axis=0, dtype=jnp.float32)
        grad_w_outer = product(active, grad_y, "tf,td->fd")
        grad_active = product(grad_y, w_outer, "td,fd->tf")
        gelu_back = jax.vjp(jax.nn.gelu, inner)[1]
        grad_inner = gelu_back(grad_active)[0].astype(jnp.bfloat16)
        grad_b_inner = jnp.sum(grad_inner, axis=0, dtype=jnp.float32)
        grad_w_inner = product(normed_two, grad_inner, "td,tf->df")
        grad_normed_two = product(grad_inner, w_inner, "tf,df->td").reshape(after.shape)
        norm_back_two = jax.vjp(
            layer_norm, after, gain_m.astype(jnp.float32), shift_m.astype(jnp.float32)
        )[1]
        after_part, grad_gain_m, grad_shift_m = norm_back_two(grad_normed_two)
        grad_after = grad_hidden + after_part
        grad_attn = grad_after.astype(jnp.bfloat16).reshape(-1, width)
        grad_w_output = product(mixed, grad_attn, "tc,td->cd")
        grad_mixed = (
            product(grad_attn, w_output, "td,cd->tc")
            .astype(jnp.bfloat16)
            .reshape(seq_dev, local_len, heads, head)
        )
        backward_scores, backward_select = score_block(backward_query, backward_keys_whole)
        probs = jnp.exp(logits_from(backward_scores, backward_select, backward_before) - log_total)
        values_heads = values_whole.reshape(seq_dev, full_len, heads, head)
        grad_probs = product(grad_mixed, values_heads, "sqhe,skhe->shqk")
        delta = jnp.sum(probs * grad_probs, axis=-1, keepdims=True)
        grad_logits = probs * (grad_probs - delta)
        grad_carried = -jnp.sum(grad_logits, axis=1)
        column_back = jnp.sum(grad_carried, axis=1)
        later_rows, _ = line_prefix(column_back, "seq", True)
        grad_select = later_rows[:, None, :] + jnp.einsum(
            "qr,sqk->srk", strict_lower, grad_carried, precision=highest
        )
        grad_first = jnp.where(
            select_mask & (backward_scores[:, 0] > 0.0), grad_select * select_scale, 0.0
        )
        grad_scores = grad_logits.at[:, 0].add(grad_first).astype(jnp.bfloat16)
        grad_query = (
            (
                product(
                    grad_scores,
                    backward_keys_whole.reshape(seq_dev, full_len, heads, head),
                    "shqk,skhe->sqhe",
                )
                * 0.125
            )
            .astype(jnp.bfloat16)
            .reshape(-1, width)
        )
        grad_values = product(probs.astype(jnp.bfloat16), grad_mixed, "shqk,sqhe->skhe")
        key_part = (product(grad_scores, backward_query, "shqk,sqhe->skhe") * 0.125).reshape(
            seq_dev, full_len, width
        )
        grad_keys = scatter_line(
            key_part.astype(jnp.bfloat16)
            .reshape(seq_dev, seq_count, local_len, width)
            .transpose(1, 0, 2, 3),
            "seq",
        )
        grad_vals = scatter_line(
            grad_values.astype(jnp.bfloat16)
            .reshape(seq_dev, seq_count, local_len, width)
            .transpose(1, 0, 2, 3),
            "seq",
        )
        grad_keys = grad_keys.reshape(-1, width)
        grad_vals = grad_vals.reshape(-1, width)
        grad_w_query = product(normed, grad_query, "tc,td->cd")
        grad_w_key = product(normed, grad_keys, "tc,td->cd")
        grad_w_value = product(normed, grad_vals, "tc,td->cd")
        grad_normed = (
            product(grad_query, w_query, "td,cd->tc")
            + product(grad_keys, w_key, "td,cd->tc")
            + product(grad_vals, w_value, "td,cd->tc")
        )
        norm_back_one = jax.vjp(
            layer_norm, backward_hidden, gain_a.astype(jnp.float32), shift_a.astype(jnp.float32)
        )[1]
        hidden_part, grad_gain_a, grad_shift_a = norm_back_one(
            grad_normed.reshape(backward_hidden.shape)
        )
        grad_hidden = grad_after + hidden_part
        low = jnp.bfloat16
        pieces = [
            piece.astype(low)[None]
            for piece in (grad_w_query, grad_w_key, grad_w_value, grad_w_output)
        ]
        pieces.append(grad_w_inner.astype(low).reshape(width, parts, width).transpose(1, 0, 2))
        pieces.append(pack_outer(grad_w_outer.astype(low), parts, devices))
        reduced[layer_index] = lax.psum_scatter(
            jnp.concatenate(pieces), both, scatter_dimension=1, tiled=True
        ).astype(jnp.float32)
        vector_grads[layer_index] = jnp.concatenate(
            [
                grad_gain_a,
                grad_shift_a,
                grad_gain_m,
                grad_shift_m,
                grad_b_outer,
                grad_b_inner,
            ]
        )
    count = jnp.where(is_last, jnp.sum(lengths).astype(jnp.float32), 0.0)
    flat = jnp.concatenate(
        vector_grads + [jnp.broadcast_to(share_sum, (128,)), jnp.broadcast_to(count, (128,))]
    )
    flat = sum_all(flat.reshape(-1, 128), ("seq", "dp")).reshape(-1)
    size = (5 + parts) * width
    selected = flat[layers * size] / (layers * flat[layers * size + 128])
    place = lax.axis_index("dp") * seq_count + lax.axis_index("seq")
    vec = flat[: layers * size].reshape(layers, size)

    def mine(first, length):
        return lax.dynamic_slice_in_dim(
            vec[:, first * width : first * width + length], place * (length // devices),
            length // devices, axis=1,
        )

    rows = width // devices
    stack = jnp.stack(reduced)
    grads_inner = (
        stack[:, 4 : 4 + parts].transpose(0, 2, 1, 3).reshape(layers, rows, parts * width)
    )
    grads_outer = stack[:, 4 + parts :].reshape(layers, parts * rows, width)
    return (
        hidden,
        grad_hidden,
        mine(0, width),
        mine(1, width),
        stack[:, 0],
        stack[:, 1],
        stack[:, 2],
        stack[:, 3],
        mine(2, width),
        mine(3, width),
        grads_inner,
        mine(5, parts * width),
        grads_outer,
        mine(4, width),
        selected,
    )


def solution(mesh):
    placed = (
        P("dp", "seq", None),
        P("dp"),
        P(None, ("dp", "seq")),
        P(None, ("dp", "seq")),
        P(None, ("dp", "seq"), None),
        P(None, ("dp", "seq"), None),
        P(None, ("dp", "seq"), None),
        P(None, ("dp", "seq"), None),
        P(None, ("dp", "seq")),
        P(None, ("dp", "seq")),
        P(None, ("dp", "seq"), None),
        P(None, ("dp", "seq")),
        P(None, ("dp", "seq"), None),
        P(None, ("dp", "seq")),
        P("dp", "seq", None),
    )
    return jax.shard_map(
        local,
        mesh=mesh,
        in_specs=placed,
        out_specs=(
            P("dp", "seq", None),
            P("dp", "seq", None),
            P(None, ("dp", "seq")),
            P(None, ("dp", "seq")),
            P(None, ("dp", "seq"), None),
            P(None, ("dp", "seq"), None),
            P(None, ("dp", "seq"), None),
            P(None, ("dp", "seq"), None),
            P(None, ("dp", "seq")),
            P(None, ("dp", "seq")),
            P(None, ("dp", "seq"), None),
            P(None, ("dp", "seq")),
            P(None, ("dp", "seq"), None),
            P(None, ("dp", "seq")),
            P(),
        ),
        check_vma=False,
    )
```

```python
import jax
import jax.numpy as jnp
from jax import lax
from jax.experimental import pallas as pl
from jax.experimental.pallas import tpu as pltpu
from jax.sharding import PartitionSpec as P

HEADS = 12


norm_eps = 1e-05
share_level = 0.5
select_strength = 2.0
masked_value = -1e30


def layer_norm(hidden, gain, shift):
    average = jnp.mean(hidden, axis=-1, keepdims=True)
    centered = hidden - average
    spread = jnp.mean(centered * centered, axis=-1, keepdims=True)
    return centered * lax.rsqrt(spread + norm_eps) * gain + shift


def product(left, right, form):
    return jnp.einsum(form, left, right, preferred_element_type=jnp.float32)


def flip(array, axis, bit):
    size = lax.axis_size(axis)
    return lax.ppermute(array, axis, [(i, i ^ bit) for i in range(size)])


def bits_of(axis):
    size = lax.axis_size(axis)
    return [1 << k for k in range(size.bit_length() - 1)]


def upper(axis, bit):
    return (lax.axis_index(axis) & bit) != 0


def gather_line(array, axis):
    blocks = array[None]
    for bit in reversed(bits_of(axis)):
        other = flip(blocks, axis, bit)
        is_upper = upper(axis, bit)
        low = jnp.where(is_upper, other, blocks)
        high = jnp.where(is_upper, blocks, other)
        blocks = jnp.stack([low, high])
        blocks = blocks.reshape((-1,) + array.shape)
    steps = len(bits_of(axis))
    blocks = blocks.reshape((2,) * steps + array.shape)
    order = tuple(reversed(range(steps))) + tuple(range(steps, blocks.ndim))
    return blocks.transpose(order).reshape((-1,) + array.shape)


def sum_all(array, axes):
    for axis in axes:
        for bit in bits_of(axis):
            array = array + flip(array, axis, bit)
    return array


def pack_weights(w_query, w_key, w_value, w_output, w_inner, w_outer):
    rows, width = w_query.shape
    parts = w_inner.shape[1] // width
    inner = w_inner.reshape(rows, parts, width).transpose(1, 0, 2)
    outer = w_outer.reshape(parts, rows, width)
    square = jnp.stack([w_query, w_key, w_value, w_output])
    return jnp.concatenate([square, inner, outer])


def unpack_outer(planes, devices):
    parts, rows, width = planes.shape
    split = planes.reshape(parts, devices, rows // devices, width)
    return split.transpose(1, 0, 2, 3).reshape(parts * rows, width)


def pack_outer(grad, parts, devices):
    rows, width = grad.shape
    split = grad.reshape(devices, parts, rows // (parts * devices), width)
    return split.transpose(1, 0, 2, 3).reshape(parts, rows // parts, width)


def dims_of(scalars, rows, cols):
    place = scalars[0]
    length = scalars[1]
    local = rows
    count = cols // rows
    row = place * local + lax.broadcasted_iota(jnp.int32, (rows, cols), 0)
    within = lax.broadcasted_iota(jnp.int32, (1, local), 1)
    col = jnp.concatenate([(place ^ b) * local + within for b in range(count)], axis=1)
    return row, col, length


def half(array, which):
    lane = lax.broadcasted_iota(jnp.int32, array.shape, 1)
    keep = lane < array.shape[1] // 2
    if which:
        keep = jnp.logical_not(keep)
    return jnp.where(keep, array, jnp.zeros_like(array))


def rowdot(left, right):
    return lax.dot_general(
        left, right, (((1,), (1,)), ((), ())), preferred_element_type=jnp.float32
    )


def coldot(left, right):
    return lax.dot_general(
        left, right, (((0,), (0,)), ((), ())), preferred_element_type=jnp.float32
    )


def plain(left, right):
    return jnp.dot(left, right, preferred_element_type=jnp.float32)


def triangle(rows, upper):
    first = lax.broadcasted_iota(jnp.int32, (rows, rows), 0)
    second = lax.broadcasted_iota(jnp.int32, (rows, rows), 1)
    inside = (first < second) if upper else (first > second)
    return jnp.where(inside, 1.0, 0.0).astype(jnp.bfloat16)


def exact_sums(matrix, array):
    high = array.astype(jnp.bfloat16)
    rest = array - high.astype(jnp.float32)
    mid = rest.astype(jnp.bfloat16)
    low = (rest - mid.astype(jnp.float32)).astype(jnp.bfloat16)
    return plain(matrix, high) + plain(matrix, mid) + plain(matrix, low)


def pick_kernel(scalars, q_ref, *refs):
    count = len(refs) - 2
    keys = refs[:count]
    carried_ref, column_ref = refs[count:]
    rows = q_ref.shape[0]
    cols = rows * count
    row, col, length = dims_of(scalars, rows, cols)
    query = half(q_ref[...], 0)
    scores = jnp.concatenate([rowdot(query, key[...]) for key in keys], axis=1)
    mask = (row > col) & (col >= 1) & (row < length) & (col < length)
    select = jnp.where(mask, jnp.maximum(scores, 0.0), 0.0) * (0.125 * select_strength / cols)
    carried_ref[...] = exact_sums(triangle(rows, False), select)
    column_ref[...] = jnp.sum(select, axis=0, keepdims=True)


def fill_bias(scalars, bias_ref, carried_ref, before_ref):
    rows, cols = bias_ref.shape
    row, col, length = dims_of(scalars, rows, cols)
    carried = carried_ref[...] + before_ref[...]
    bias_ref[...] = jnp.where((row >= col) & (col < length), -carried, masked_value)


CHUNK = 32


def mix_kernel(scalars, q_ref, carried_ref, before_ref, *refs):
    count = (len(refs) - 5) // 2
    keys = refs[:count]
    values = refs[count : 2 * count]
    mixed_ref, total_ref, bias_ref, score_ref, prob_ref = refs[2 * count :]
    rows = q_ref.shape[0]

    @pl.when(pl.program_id(0) == 0)
    def _():
        fill_bias(scalars, bias_ref, carried_ref, before_ref)

    outs = []
    for which in range(2):
        query = half(q_ref[...], which) * jnp.asarray(0.125, jnp.bfloat16)
        for b in range(count):
            score_ref[which, :, b * rows : (b + 1) * rows] = rowdot(query, keys[b][...])
    for which in range(2):
        for chunk in range(rows // CHUNK):
            at = slice(chunk * CHUNK, (chunk + 1) * CHUNK)
            logits = score_ref[which, at, :] + bias_ref[at, :]
            peak = jnp.max(logits, axis=1, keepdims=True)
            expo = jnp.exp(logits - peak)
            denominator = jnp.sum(expo, axis=1, keepdims=True)
            prob_ref[which, at, :] = (expo * (1.0 / denominator)).astype(jnp.bfloat16)
            total = peak + jnp.log(denominator)
            width = total_ref.shape[1] // 2
            total_ref[at, which * width : (which + 1) * width] = jnp.broadcast_to(
                total, (CHUNK, width)
            )
        acc = plain(prob_ref[which, :, 0:rows], values[0][...])
        for b in range(1, count):
            acc = acc + plain(prob_ref[which, :, b * rows : (b + 1) * rows], values[b][...])
        outs.append(acc)
    mixed_ref[...] = (half(outs[0], 0) + half(outs[1], 1)).astype(jnp.bfloat16)


def back_kernel(scalars, q_ref, dm_ref, total_ref, carried_ref, before_ref, *refs):
    count = (len(refs) - 11) // 2
    keys = refs[:count]
    values = refs[count : 2 * count]
    (
        dq_ref,
        dk_ref,
        dv_ref,
        sum_ref,
        first_ref,
        column_ref,
        bias_ref,
        score_ref,
        dprob_ref,
        prob_ref,
        ds_ref,
    ) = refs[2 * count :]
    rows = q_ref.shape[0]
    step = pl.program_id(0)

    @pl.when(step == 0)
    def _():
        fill_bias(scalars, bias_ref, carried_ref, before_ref)
        sum_ref[...] = jnp.zeros_like(sum_ref)

    eighth = jnp.asarray(0.125, jnp.bfloat16)
    queries = [half(q_ref[...], which) * eighth for which in range(2)]
    grads = [half(dm_ref[...], which) for which in range(2)]
    for which in range(2):
        for b in range(count):
            at = slice(b * rows, (b + 1) * rows)
            score_ref[which, :, at] = rowdot(queries[which], keys[b][...])
            dprob_ref[which, :, at] = rowdot(grads[which], values[b][...])
    for which in range(2):
        width = total_ref.shape[1] // 2
        for chunk in range(rows // CHUNK):
            at = slice(chunk * CHUNK, (chunk + 1) * CHUNK)
            total = total_ref[at, which * width : which * width + 1]
            probs = jnp.exp(score_ref[which, at, :] + bias_ref[at, :] - total)
            dprob = dprob_ref[which, at, :]
            delta = jnp.sum(probs * dprob, axis=1, keepdims=True)
            dlogits = probs * (dprob - delta)
            prob_ref[which, at, :] = probs.astype(jnp.bfloat16)
            sum_ref[at, :] = sum_ref[at, :] + dlogits
            ds_ref[which, at, :] = dlogits.astype(jnp.bfloat16)
            if which == 0:

                @pl.when(step == 0)
                def _():
                    first_ref[at, :] = dlogits

    @pl.when(step == 0)
    def _():
        ds_ref[0] = jnp.zeros_like(ds_ref[0])

    dq = []
    for which in range(2):
        acc = plain(ds_ref[which, :, 0:rows], keys[0][...])
        for b in range(1, count):
            acc = acc + plain(ds_ref[which, :, b * rows : (b + 1) * rows], keys[b][...])
        dq.append(acc)
    dq_ref[...] = ((half(dq[0], 0) + half(dq[1], 1)) * 0.125).astype(jnp.bfloat16)
    for b in range(count):
        at = slice(b * rows, (b + 1) * rows)
        dk = coldot(ds_ref[0, :, at], queries[0]) + coldot(ds_ref[1, :, at], queries[1])
        dv = coldot(prob_ref[0, :, at], grads[0]) + coldot(prob_ref[1, :, at], grads[1])
        dk_ref[b] = dk.astype(jnp.bfloat16)
        dv_ref[b] = dv.astype(jnp.bfloat16)

    @pl.when(step == pl.num_programs(0) - 1)
    def _():
        column_ref[...] = jnp.sum(sum_ref[...], axis=0, keepdims=True)


def first_kernel(scalars, q_ref, sum_ref, first_ref, later_ref, dq_in, dk_in, *refs):
    count = len(refs) - 2
    keys = refs[:count]
    dq_ref, dk_ref = refs[count:]
    rows = q_ref.shape[0]
    cols = rows * count
    row, col, length = dims_of(scalars, rows, cols)
    query = half(q_ref[...], 0)
    scores = jnp.concatenate([rowdot(query, key[...]) for key in keys], axis=1)
    mask = (row > col) & (col >= 1) & (row < length) & (col < length) & (scores > 0.0)
    later = exact_sums(triangle(rows, True), sum_ref[...]) + later_ref[...]
    extra = jnp.where(mask, later, 0.0) * (-select_strength / cols)
    dscores = (first_ref[...] + extra).astype(jnp.bfloat16)
    acc = plain(dscores[:, 0:rows], keys[0][...])
    for b in range(1, count):
        acc = acc + plain(dscores[:, b * rows : (b + 1) * rows], keys[b][...])
    dq_ref[...] = dq_in[...] + half(acc * 0.125, 0).astype(jnp.bfloat16)
    scaled = query * jnp.asarray(0.125, jnp.bfloat16)
    for b in range(count):
        dk = coldot(dscores[:, b * rows : (b + 1) * rows], scaled)
        dk_ref[b] = dk_in[b] + dk.astype(jnp.bfloat16)


PAIR = 128


def pick(scalars, query, keys):
    rows, width = query.shape
    cols = rows * len(keys)
    one = pl.BlockSpec((rows, PAIR), lambda h, s: (0, 0))
    return pl.pallas_call(
        pick_kernel,
        name="pick",
        out_shape=(
            jax.ShapeDtypeStruct((rows, cols), jnp.float32),
            jax.ShapeDtypeStruct((1, cols), jnp.float32),
        ),
        grid_spec=pltpu.PrefetchScalarGridSpec(
            num_scalar_prefetch=1,
            grid=(1,),
            in_specs=[one] * (1 + len(keys)),
            out_specs=(
                pl.BlockSpec((rows, cols), lambda h, s: (0, 0)),
                pl.BlockSpec((1, cols), lambda h, s: (0, 0)),
            ),
        ),
    )(scalars, query, *keys)


def mix(scalars, query, carried, before, keys, values):
    rows, width = query.shape
    cols = rows * len(keys)
    pair = pl.BlockSpec((rows, PAIR), lambda h, s: (0, h))
    full = pl.BlockSpec((rows, cols), lambda h, s: (0, 0))
    line = pl.BlockSpec((1, cols), lambda h, s: (0, 0))
    return pl.pallas_call(
        mix_kernel,
        name="mix",
        out_shape=(
            jax.ShapeDtypeStruct((rows, width), jnp.bfloat16),
            jax.ShapeDtypeStruct((rows, width), jnp.float32),
        ),
        grid_spec=pltpu.PrefetchScalarGridSpec(
            num_scalar_prefetch=1,
            grid=(width // PAIR,),
            in_specs=[pair, full, line] + [pair] * (2 * len(keys)),
            out_specs=(pair, pair),
            scratch_shapes=[
                pltpu.VMEM((rows, cols), jnp.float32),
                pltpu.VMEM((2, rows, cols), jnp.float32),
                pltpu.VMEM((2, rows, cols), jnp.bfloat16),
            ],
        ),
    )(scalars, query, carried, before, *keys, *values)


def back(scalars, query, grad_mixed, total, carried, before, keys, values):
    rows, width = query.shape
    count = len(keys)
    cols = rows * count
    pair = pl.BlockSpec((rows, PAIR), lambda h, s: (0, h))
    full = pl.BlockSpec((rows, cols), lambda h, s: (0, 0))
    line = pl.BlockSpec((1, cols), lambda h, s: (0, 0))
    blocks = pl.BlockSpec((count, rows, PAIR), lambda h, s: (0, 0, h))
    return pl.pallas_call(
        back_kernel,
        name="back",
        out_shape=(
            jax.ShapeDtypeStruct((rows, width), jnp.bfloat16),
            jax.ShapeDtypeStruct((count, rows, width), jnp.bfloat16),
            jax.ShapeDtypeStruct((count, rows, width), jnp.bfloat16),
            jax.ShapeDtypeStruct((rows, cols), jnp.float32),
            jax.ShapeDtypeStruct((rows, cols), jnp.float32),
            jax.ShapeDtypeStruct((1, cols), jnp.float32),
        ),
        grid_spec=pltpu.PrefetchScalarGridSpec(
            num_scalar_prefetch=1,
            grid=(width // PAIR,),
            in_specs=[pair, pair, pair, full, line] + [pair] * (2 * count),
            out_specs=(pair, blocks, blocks, full, full, line),
            scratch_shapes=[
                pltpu.VMEM((rows, cols), jnp.float32),
                pltpu.VMEM((2, rows, cols), jnp.float32),
                pltpu.VMEM((2, rows, cols), jnp.float32),
                pltpu.VMEM((2, rows, cols), jnp.bfloat16),
                pltpu.VMEM((2, rows, cols), jnp.bfloat16),
            ],
        ),
    )(scalars, query, grad_mixed, total, carried, before, *keys, *values)


def first(scalars, query, sums, first_logits, later, dq, dk, keys):
    rows, width = query.shape
    count = len(keys)
    cols = rows * count
    one = pl.BlockSpec((rows, PAIR), lambda h, s: (0, 0))
    full = pl.BlockSpec((rows, cols), lambda h, s: (0, 0))
    line = pl.BlockSpec((1, cols), lambda h, s: (0, 0))
    blocks = pl.BlockSpec((count, rows, PAIR), lambda h, s: (0, 0, 0))
    return pl.pallas_call(
        first_kernel,
        name="first",
        out_shape=(
            jax.ShapeDtypeStruct((rows, width), jnp.bfloat16),
            jax.ShapeDtypeStruct((count, rows, width), jnp.bfloat16),
        ),
        grid_spec=pltpu.PrefetchScalarGridSpec(
            num_scalar_prefetch=1,
            grid=(1,),
            in_specs=[one, full, full, line, one, blocks] + [one] * count,
            out_specs=(one, blocks),
        ),
        input_output_aliases={5: 0, 6: 1},
    )(scalars, query, sums, first_logits, later, dq, dk, *keys)


def spread(array, axis):
    size = lax.axis_size(axis)
    got = {0: array}
    for bit in reversed(bits_of(axis)):
        for b in list(got):
            got[b ^ bit] = flip(got[b], axis, bit)
    return [got[b] for b in range(size)]


def collect(blocks, axis):
    for bit in bits_of(axis):
        size = blocks.shape[0] // 2
        pairs = blocks.reshape((size, 2) + blocks.shape[1:])
        blocks = pairs[:, 0] + flip(pairs[:, 1], axis, bit)
    return blocks[0]


def line_prefix(array, axis, reverse):
    size = array.shape[0]
    total = array
    before = jnp.zeros_like(array)
    for bit in bits_of(axis):
        other = flip(total, axis, bit)
        other = jnp.stack([other[b ^ bit] for b in range(size)])
        is_upper = upper(axis, bit)
        take = jnp.logical_not(is_upper) if reverse else is_upper
        before = before + jnp.where(take, other, 0.0)
        total = total + other
    return before, total


def local(
    inputs,
    lengths,
    gain_attend,
    shift_attend,
    weight_query,
    weight_key,
    weight_value,
    weight_output,
    gain_mixer,
    shift_mixer,
    weight_inner,
    bias_inner,
    weight_outer,
    bias_outer,
    cotangent,
):
    layers = gain_attend.shape[0]
    seq_dev, local_len, width = inputs.shape
    seq_count = lax.axis_size("seq")
    devices = lax.axis_size(("dp", "seq"))
    is_last = lax.axis_index("seq") == seq_count - 1
    place = lax.axis_index("seq")
    key_place = (place ^ jnp.arange(seq_count, dtype=jnp.int32))[:, None] * local_len + jnp.arange(
        local_len, dtype=jnp.int32
    )
    valid_keys = key_place < lengths[0]
    scalars = jnp.stack([place, lengths[0]]).astype(jnp.int32)
    both = ("dp", "seq")
    parts = weight_inner.shape[2] // width
    vectors = jnp.concatenate(
        [gain_attend, shift_attend, gain_mixer, shift_mixer, bias_outer, bias_inner], axis=1
    )
    vector_rows = gather_line(gather_line(vectors, "seq"), "dp")
    per = width // devices
    vector_rows = vector_rows.reshape(devices, layers, -1)
    small = [
        vector_rows[:, :, k * per : (k + 1) * per].transpose(1, 0, 2).reshape(layers, width)
        for k in range(5)
    ]
    small.append(
        vector_rows[:, :, 5 * per :].transpose(1, 0, 2).reshape(layers, parts * width)
    )
    whole = [
        lax.all_gather(
            pack_weights(
                weight_query[k],
                weight_key[k],
                weight_value[k],
                weight_output[k],
                weight_inner[k],
                weight_outer[k],
            ),
            both,
            axis=1,
            tiled=True,
        )
        for k in range(layers)
    ]
    w_outers = [unpack_outer(planes[4 + parts :], devices) for planes in whole]

    hidden = inputs.astype(jnp.float32)
    share_sum = jnp.zeros((), jnp.float32)
    saved = []
    for layer_index in range(layers):
        planes = whole[layer_index]
        forward_gain_a, forward_shift_a, forward_gain_m, forward_shift_m = (
            small[k][layer_index] for k in range(4)
        )
        forward_b_outer, forward_b_inner = (small[k][layer_index] for k in (4, 5))
        forward_w_query, forward_w_key, forward_w_value, forward_w_output = (
            planes[k] for k in range(4)
        )
        forward_w_inner = planes[4 : 4 + parts].transpose(1, 0, 2).reshape(width, parts * width)
        forward_w_outer = w_outers[layer_index]
        forward_normed = (
            layer_norm(
                hidden, forward_gain_a.astype(jnp.float32), forward_shift_a.astype(jnp.float32)
            )
            .astype(jnp.bfloat16)
            .reshape(-1, width)
        )
        forward_keys = jnp.dot(
            forward_normed, forward_w_key, preferred_element_type=jnp.float32
        ).astype(jnp.bfloat16)
        forward_query = jnp.dot(
            forward_normed, forward_w_query, preferred_element_type=jnp.float32
        ).astype(jnp.bfloat16)
        forward_values = jnp.dot(
            forward_normed, forward_w_value, preferred_element_type=jnp.float32
        ).astype(jnp.bfloat16)
        all_keys = spread(forward_keys, "seq")
        all_values = spread(forward_values, "seq")
        carried, column = pick(scalars, forward_query, all_keys)
        before, totals = line_prefix(column.reshape(seq_count, local_len), "seq", False)
        before = before.reshape(1, -1)
        forward_mixed, log_total = mix(
            scalars, forward_query, carried, before, all_keys, all_values
        )
        forward_after = hidden + jnp.dot(
            forward_mixed, forward_w_output, preferred_element_type=jnp.float32
        ).reshape(hidden.shape)
        forward_normed_two = (
            layer_norm(
                forward_after,
                forward_gain_m.astype(jnp.float32),
                forward_shift_m.astype(jnp.float32),
            )
            .astype(jnp.bfloat16)
            .reshape(-1, width)
        )
        forward_inner = jnp.dot(
            forward_normed_two, forward_w_inner, preferred_element_type=jnp.float32
        ) + forward_b_inner.astype(jnp.float32)
        forward_active = jax.nn.gelu(forward_inner).astype(jnp.bfloat16)
        outer = jnp.dot(
            forward_active, forward_w_outer, preferred_element_type=jnp.float32
        ) + forward_b_outer.astype(jnp.float32)
        result = forward_after + outer.reshape(hidden.shape)
        share = jnp.where(
            is_last,
            jnp.sum(jnp.where(valid_keys, jnp.minimum(totals / share_level, 1.0), 0.0)),
            0.0,
        )
        forward_kept = (
            hidden,
            forward_normed,
            forward_query,
            all_keys,
            all_values,
            carried,
            before,
            log_total,
            forward_mixed,
            forward_after,
            forward_normed_two,
            forward_inner,
            forward_active,
        )
        hidden = result
        share_sum = share_sum + share
        saved.append(forward_kept)
    grad_hidden = cotangent
    reduced = [None] * layers
    vector_grads = [None] * layers
    for layer_index in reversed(range(layers)):
        planes = whole[layer_index]
        gain_a, shift_a, gain_m, shift_m = (small[k][layer_index] for k in range(4))
        w_query, w_key, w_value, w_output = (planes[k] for k in range(4))
        w_inner = planes[4 : 4 + parts].transpose(1, 0, 2).reshape(width, parts * width)
        w_outer = w_outers[layer_index]
        (
            backward_hidden,
            normed,
            backward_query,
            all_keys,
            all_values,
            carried,
            before,
            log_total,
            mixed,
            after,
            normed_two,
            inner,
            active,
        ) = saved[layer_index]
        grad_y = grad_hidden.astype(jnp.bfloat16).reshape(-1, width)
        grad_b_outer = jnp.sum(grad_y, axis=0, dtype=jnp.float32)
        grad_w_outer = product(active, grad_y, "tf,td->fd")
        grad_active = product(grad_y, w_outer, "td,fd->tf")
        gelu_back = jax.vjp(jax.nn.gelu, inner)[1]
        grad_inner = gelu_back(grad_active)[0].astype(jnp.bfloat16)
        grad_b_inner = jnp.sum(grad_inner, axis=0, dtype=jnp.float32)
        grad_w_inner = product(normed_two, grad_inner, "td,tf->df")
        grad_normed_two = product(grad_inner, w_inner, "tf,df->td").reshape(after.shape)
        norm_back_two = jax.vjp(
            layer_norm, after, gain_m.astype(jnp.float32), shift_m.astype(jnp.float32)
        )[1]
        after_part, grad_gain_m, grad_shift_m = norm_back_two(grad_normed_two)
        grad_after = grad_hidden + after_part
        grad_attn = grad_after.astype(jnp.bfloat16).reshape(-1, width)
        grad_w_output = product(mixed, grad_attn, "tc,td->cd")
        grad_mixed = product(grad_attn, w_output, "td,cd->tc").astype(jnp.bfloat16)
        grad_query, key_part, value_part, sums, first_logits, column_back = back(
            scalars, backward_query, grad_mixed, log_total, carried, before, all_keys, all_values
        )
        grad_vals = collect(value_part, "seq")
        later, _ = line_prefix(column_back.reshape(seq_count, local_len), "seq", True)
        grad_query, key_part = first(
            scalars,
            backward_query,
            sums,
            first_logits,
            later.reshape(1, -1),
            grad_query,
            key_part,
            all_keys,
        )
        grad_keys = collect(key_part, "seq")
        grad_w_query = product(normed, grad_query, "tc,td->cd")
        grad_w_key = product(normed, grad_keys, "tc,td->cd")
        grad_w_value = product(normed, grad_vals, "tc,td->cd")
        grad_normed = (
            product(grad_query, w_query, "td,cd->tc")
            + product(grad_keys, w_key, "td,cd->tc")
            + product(grad_vals, w_value, "td,cd->tc")
        )
        norm_back_one = jax.vjp(
            layer_norm, backward_hidden, gain_a.astype(jnp.float32), shift_a.astype(jnp.float32)
        )[1]
        hidden_part, grad_gain_a, grad_shift_a = norm_back_one(
            grad_normed.reshape(backward_hidden.shape)
        )
        grad_hidden = grad_after + hidden_part
        low = jnp.bfloat16
        pieces = [
            piece.astype(low)[None]
            for piece in (grad_w_query, grad_w_key, grad_w_value, grad_w_output)
        ]
        pieces.append(grad_w_inner.astype(low).reshape(width, parts, width).transpose(1, 0, 2))
        pieces.append(pack_outer(grad_w_outer.astype(low), parts, devices))
        reduced[layer_index] = lax.psum_scatter(
            jnp.concatenate(pieces), both, scatter_dimension=1, tiled=True
        ).astype(jnp.float32)
        vector_grads[layer_index] = jnp.concatenate(
            [
                grad_gain_a,
                grad_shift_a,
                grad_gain_m,
                grad_shift_m,
                grad_b_outer,
                grad_b_inner,
            ]
        )
    count = jnp.where(is_last, jnp.sum(lengths).astype(jnp.float32), 0.0)
    flat = jnp.concatenate(
        vector_grads + [jnp.broadcast_to(share_sum, (128,)), jnp.broadcast_to(count, (128,))]
    )
    flat = sum_all(flat.reshape(-1, 128), ("seq", "dp")).reshape(-1)
    size = (5 + parts) * width
    selected = flat[layers * size] / (layers * flat[layers * size + 128])
    place_of = lax.axis_index("dp") * seq_count + place
    vec = flat[: layers * size].reshape(layers, size)

    def mine(first, length):
        return lax.dynamic_slice_in_dim(
            vec[:, first * width : first * width + length], place_of * (length // devices),
            length // devices, axis=1,
        )

    rows = width // devices
    stack = jnp.stack(reduced)
    grads_inner = (
        stack[:, 4 : 4 + parts].transpose(0, 2, 1, 3).reshape(layers, rows, parts * width)
    )
    grads_outer = stack[:, 4 + parts :].reshape(layers, parts * rows, width)
    return (
        hidden,
        grad_hidden,
        mine(0, width),
        mine(1, width),
        stack[:, 0],
        stack[:, 1],
        stack[:, 2],
        stack[:, 3],
        mine(2, width),
        mine(3, width),
        grads_inner,
        mine(5, parts * width),
        grads_outer,
        mine(4, width),
        selected,
    )


def solution(mesh):
    placed = (
        P("dp", "seq", None),
        P("dp"),
        P(None, ("dp", "seq")),
        P(None, ("dp", "seq")),
        P(None, ("dp", "seq"), None),
        P(None, ("dp", "seq"), None),
        P(None, ("dp", "seq"), None),
        P(None, ("dp", "seq"), None),
        P(None, ("dp", "seq")),
        P(None, ("dp", "seq")),
        P(None, ("dp", "seq"), None),
        P(None, ("dp", "seq")),
        P(None, ("dp", "seq"), None),
        P(None, ("dp", "seq")),
        P("dp", "seq", None),
    )
    return jax.shard_map(
        local,
        mesh=mesh,
        in_specs=placed,
        out_specs=(
            P("dp", "seq", None),
            P("dp", "seq", None),
            P(None, ("dp", "seq")),
            P(None, ("dp", "seq")),
            P(None, ("dp", "seq"), None),
            P(None, ("dp", "seq"), None),
            P(None, ("dp", "seq"), None),
            P(None, ("dp", "seq"), None),
            P(None, ("dp", "seq")),
            P(None, ("dp", "seq")),
            P(None, ("dp", "seq"), None),
            P(None, ("dp", "seq")),
            P(None, ("dp", "seq"), None),
            P(None, ("dp", "seq")),
            P(),
        ),
        check_vma=False,
    )
```

```python
import jax
import jax.numpy as jnp
from jax import lax
from jax.experimental import pallas as pl
from jax.experimental.pallas import tpu as pltpu
from jax.sharding import PartitionSpec as P

HEADS = 12


norm_eps = 1e-05
share_level = 0.5
select_strength = 2.0
masked_value = -1e30


def layer_norm(hidden, gain, shift):
    average = jnp.mean(hidden, axis=-1, keepdims=True)
    centered = hidden - average
    spread = jnp.mean(centered * centered, axis=-1, keepdims=True)
    return centered * lax.rsqrt(spread + norm_eps) * gain + shift


def product(left, right, form):
    return jnp.einsum(form, left, right, preferred_element_type=jnp.float32)


def flip(array, axis, bit):
    size = lax.axis_size(axis)
    return lax.ppermute(array, axis, [(i, i ^ bit) for i in range(size)])


def bits_of(axis):
    size = lax.axis_size(axis)
    return [1 << k for k in range(size.bit_length() - 1)]


def upper(axis, bit):
    return (lax.axis_index(axis) & bit) != 0


def sum_all(array, axes):
    for axis in axes:
        for bit in bits_of(axis):
            array = array + flip(array, axis, bit)
    return array


def reduce_blocks(planes, steps):
    count, rows, width = planes.shape
    dims = [("dp", bit) for bit in reversed(bits_of("dp"))]
    dims += [("seq", bit) for bit in reversed(bits_of("seq"))]
    blocks = planes.reshape((count,) + (2,) * len(dims) + (rows >> len(dims), width))
    for step in steps:
        axis, bit = step
        dim = 1 + dims.index(step)
        mine = upper(axis, bit).astype(jnp.int32)
        keep = lax.dynamic_index_in_dim(blocks, mine, dim, False)
        send = lax.dynamic_index_in_dim(blocks, 1 - mine, dim, False)
        blocks = keep + flip(send, axis, bit)
        dims.remove(step)
    return blocks


def step_orders():
    near = [("seq", bit) for bit in bits_of("seq")][:1]
    across = [("seq", bit) for bit in bits_of("seq")][1:]
    beside = [("dp", bit) for bit in bits_of("dp")][:1]
    along = [("dp", bit) for bit in bits_of("dp")][1:]
    return (
        near + along + beside + across,
        near + beside + across + along,
        near + across + beside + along,
    )


def gather_blocks(array, steps):
    dims = []
    blocks = array
    for axis, bit in steps:
        other = flip(blocks, axis, bit)
        is_upper = upper(axis, bit)
        low = jnp.where(is_upper, other, blocks)
        high = jnp.where(is_upper, blocks, other)
        blocks = jnp.stack([low, high])
        dims.insert(0, (axis, bit))
    want = [("dp", bit) for bit in reversed(bits_of("dp"))]
    want += [("seq", bit) for bit in reversed(bits_of("seq"))]
    order = [dims.index(step) for step in want]
    blocks = blocks.transpose(order + [len(order), len(order) + 1])
    return blocks.reshape((-1,) + array.shape)


def one_hot(shape, hit):
    first = lax.broadcasted_iota(jnp.int32, shape, 0)
    second = lax.broadcasted_iota(jnp.int32, shape, 1)
    return jnp.where(hit(first, second), 1.0, 0.0).astype(jnp.bfloat16)


def pack_kernel(*refs):
    w_query, w_key, w_value, w_output, w_inner, w_outer = refs[:6]
    outs = refs[6:]
    layers, rows, width = w_query.shape
    parts = w_inner.shape[2] // width
    lane = width // 6
    span = lane * parts
    order = one_hot((span, span), lambda a, b: a == parts * (b % lane) + b // lane)
    for k in range(layers):
        out = outs[k]
        at = 0
        out[:, at : at + width] = w_output[k]
        at = width
        for w in range(6):
            moved = plain(w_inner[k, :, w * span : (w + 1) * span], order).astype(jnp.bfloat16)
            for c in range(parts):
                start = at + c * width + w * lane
                out[:, start : start + lane] = moved[:, c * lane : (c + 1) * lane]
        at = at + parts * width
        for c in range(parts):
            take = one_hot((rows, parts * rows), lambda a, b, c=c: b == parts * a + c)
            out[:, at : at + width] = plain(take, w_outer[k]).astype(jnp.bfloat16)
            at = at + width
        if k + 1 < layers:
            for square in (w_query, w_key, w_value):
                out[:, at : at + width] = square[k + 1]
                at = at + width


def pack(*weights):
    layers, rows, width = weights[0].shape
    parts = weights[4].shape[2] // width
    count = 1 + 2 * parts
    return pl.pallas_call(
        pack_kernel,
        name="pack",
        out_shape=tuple(
            jax.ShapeDtypeStruct(
                (rows, (count + (3 if k + 1 < layers else 0)) * width), jnp.bfloat16
            )
            for k in range(layers)
        ),
    )(*weights)


def spread_inner(grads, out, parts):
    lane = grads.shape[1] // (6 * parts)
    span = lane * parts
    order = one_hot((span, span), lambda a, b: b == parts * (a % lane) + a // lane)
    for w in range(6):
        pieces = [grads[:, (c * 6 + w) * lane : (c * 6 + w + 1) * lane] for c in range(parts)]
        out[:, w * span : (w + 1) * span] = plain(jnp.concatenate(pieces, axis=1), order)


def finish_kernel(late_ref, early_ref, one_ref, two_ref, three_ref, *outs):
    g_query, g_key, g_value, g_output, g_inner, g_outer = outs
    rows = late_ref.shape[0]
    width = g_query.shape[2]
    parts = g_inner.shape[2] // width
    g_query[0] = three_ref[0].astype(jnp.float32)
    g_key[0] = three_ref[1].astype(jnp.float32)
    g_value[0] = two_ref[0].astype(jnp.float32)
    g_output[0] = one_ref[0].astype(jnp.float32)
    g_query[1] = late_ref[:, :width].astype(jnp.float32)
    g_key[1] = late_ref[:, width : 2 * width].astype(jnp.float32)
    g_value[1] = two_ref[1].astype(jnp.float32)
    g_output[1] = one_ref[1].astype(jnp.float32)
    for k, ref, at in ((0, late_ref, 2 * width), (1, early_ref, 0)):
        spread_inner(ref[:, at : at + parts * width], g_inner.at[k], parts)
        at = at + parts * width
        total = 0.0
        for c in range(parts):
            put = one_hot((parts * rows, rows), lambda a, b, c=c: a == parts * b + c)
            total = total + plain(put, ref[:, at + c * width : at + (c + 1) * width])
        g_outer[k] = total


def finish(late, early, one, two, three, width, parts):
    rows = late.shape[0]
    square = jax.ShapeDtypeStruct((2, rows, width), jnp.float32)
    return pl.pallas_call(
        finish_kernel,
        name="finish",
        out_shape=(square,) * 4
        + (
            jax.ShapeDtypeStruct((2, rows, parts * width), jnp.float32),
            jax.ShapeDtypeStruct((2, parts * rows, width), jnp.float32),
        ),
    )(late, early, one, two, three)


def dims_of(scalars, rows, cols):
    place = scalars[0]
    length = scalars[1]
    local = rows
    count = cols // rows
    row = place * local + lax.broadcasted_iota(jnp.int32, (rows, cols), 0)
    within = lax.broadcasted_iota(jnp.int32, (1, local), 1)
    col = jnp.concatenate([(place ^ b) * local + within for b in range(count)], axis=1)
    return row, col, length


def half(array, which):
    lane = lax.broadcasted_iota(jnp.int32, array.shape, 1)
    keep = lane < array.shape[1] // 2
    if which:
        keep = jnp.logical_not(keep)
    return jnp.where(keep, array, jnp.zeros_like(array))


def rowdot(left, right):
    return lax.dot_general(
        left, right, (((1,), (1,)), ((), ())), preferred_element_type=jnp.float32
    )


def coldot(left, right):
    return lax.dot_general(
        left, right, (((0,), (0,)), ((), ())), preferred_element_type=jnp.float32
    )


def plain(left, right):
    return jnp.dot(left, right, preferred_element_type=jnp.float32)


def triangle(rows, upper):
    first = lax.broadcasted_iota(jnp.int32, (rows, rows), 0)
    second = lax.broadcasted_iota(jnp.int32, (rows, rows), 1)
    inside = (first < second) if upper else (first > second)
    return jnp.where(inside, 1.0, 0.0).astype(jnp.bfloat16)


def exact_sums(matrix, array):
    high = array.astype(jnp.bfloat16)
    rest = array - high.astype(jnp.float32)
    mid = rest.astype(jnp.bfloat16)
    low = (rest - mid.astype(jnp.float32)).astype(jnp.bfloat16)
    return plain(matrix, high) + plain(matrix, mid) + plain(matrix, low)


def pick_kernel(scalars, q_ref, *refs):
    count = len(refs) - 2
    keys = refs[:count]
    carried_ref, column_ref = refs[count:]
    rows = q_ref.shape[0]
    cols = rows * count
    row, col, length = dims_of(scalars, rows, cols)
    query = half(q_ref[...], 0)
    scores = jnp.concatenate([rowdot(query, key[...]) for key in keys], axis=1)
    mask = (row > col) & (col >= 1) & (row < length) & (col < length)
    select = jnp.where(mask, jnp.maximum(scores, 0.0), 0.0) * (0.125 * select_strength / cols)
    carried_ref[...] = exact_sums(triangle(rows, False), select)
    column_ref[...] = jnp.sum(select, axis=0, keepdims=True)


def fill_bias(scalars, bias_ref, carried_ref, before_ref):
    rows, cols = bias_ref.shape
    row, col, length = dims_of(scalars, rows, cols)
    carried = carried_ref[...] + before_ref[...]
    bias_ref[...] = jnp.where((row >= col) & (col < length), -carried, masked_value)


CHUNK = 32


def mix_kernel(scalars, q_ref, carried_ref, before_ref, *refs):
    count = (len(refs) - 5) // 2
    keys = refs[:count]
    values = refs[count : 2 * count]
    mixed_ref, total_ref, bias_ref, score_ref, prob_ref = refs[2 * count :]
    rows = q_ref.shape[0]

    @pl.when(pl.program_id(0) == 0)
    def _():
        fill_bias(scalars, bias_ref, carried_ref, before_ref)

    outs = []
    for which in range(2):
        query = half(q_ref[...], which) * jnp.asarray(0.125, jnp.bfloat16)
        for b in range(count):
            score_ref[which, :, b * rows : (b + 1) * rows] = rowdot(query, keys[b][...])
    for which in range(2):
        for chunk in range(rows // CHUNK):
            at = slice(chunk * CHUNK, (chunk + 1) * CHUNK)
            logits = score_ref[which, at, :] + bias_ref[at, :]
            peak = jnp.max(logits, axis=1, keepdims=True)
            expo = jnp.exp(logits - peak)
            denominator = jnp.sum(expo, axis=1, keepdims=True)
            prob_ref[which, at, :] = (expo * (1.0 / denominator)).astype(jnp.bfloat16)
            total = peak + jnp.log(denominator)
            width = total_ref.shape[1] // 2
            total_ref[at, which * width : (which + 1) * width] = jnp.broadcast_to(
                total, (CHUNK, width)
            )
        acc = plain(prob_ref[which, :, 0:rows], values[0][...])
        for b in range(1, count):
            acc = acc + plain(prob_ref[which, :, b * rows : (b + 1) * rows], values[b][...])
        outs.append(acc)
    mixed_ref[...] = (half(outs[0], 0) + half(outs[1], 1)).astype(jnp.bfloat16)


def back_kernel(scalars, q_ref, dm_ref, total_ref, carried_ref, before_ref, *refs):
    count = (len(refs) - 12) // 2
    keys = refs[:count]
    values = refs[count : 2 * count]
    (
        dq_ref,
        dk_ref,
        dv_ref,
        sum_ref,
        first_ref,
        column_ref,
        bias_ref,
        score_ref,
        dprob_ref,
        prob_ref,
        ds_ref,
        head_ref,
    ) = refs[2 * count :]
    rows = q_ref.shape[0]
    step = pl.program_id(0)

    @pl.when(step == 0)
    def _():
        fill_bias(scalars, bias_ref, carried_ref, before_ref)
        sum_ref[...] = jnp.zeros_like(sum_ref)

    later_heads = jnp.where(step == 0, 0.0, 1.0)
    eighth = jnp.asarray(0.125, jnp.bfloat16)
    queries = [half(q_ref[...], which) * eighth for which in range(2)]
    grads = [half(dm_ref[...], which) for which in range(2)]
    for which in range(2):
        for b in range(count):
            at = slice(b * rows, (b + 1) * rows)
            score_ref[which, :, at] = rowdot(queries[which], keys[b][...])
            dprob_ref[which, :, at] = rowdot(grads[which], values[b][...])
    for which in range(2):
        width = total_ref.shape[1] // 2
        for chunk in range(rows // CHUNK):
            at = slice(chunk * CHUNK, (chunk + 1) * CHUNK)
            total = total_ref[at, which * width : which * width + 1]
            probs = jnp.exp(score_ref[which, at, :] + bias_ref[at, :] - total)
            dprob = dprob_ref[which, at, :]
            delta = jnp.sum(probs * dprob, axis=1, keepdims=True)
            dlogits = probs * (dprob - delta)
            prob_ref[which, at, :] = probs.astype(jnp.bfloat16)
            sum_ref[at, :] = sum_ref[at, :] + dlogits
            if which == 0:
                head_ref[at, :] = dlogits
                dlogits = dlogits * later_heads
            ds_ref[which, at, :] = dlogits.astype(jnp.bfloat16)

    dq = []
    for which in range(2):
        acc = plain(ds_ref[which, :, 0:rows], keys[0][...])
        for b in range(1, count):
            acc = acc + plain(ds_ref[which, :, b * rows : (b + 1) * rows], keys[b][...])
        dq.append(acc)
    dq_ref[...] = ((half(dq[0], 0) + half(dq[1], 1)) * 0.125).astype(jnp.bfloat16)
    for b in range(count):
        at = slice(b * rows, (b + 1) * rows)
        dk = coldot(ds_ref[0, :, at], queries[0]) + coldot(ds_ref[1, :, at], queries[1])
        dv = coldot(prob_ref[0, :, at], grads[0]) + coldot(prob_ref[1, :, at], grads[1])
        dk_ref[b] = dk.astype(jnp.bfloat16)
        dv_ref[b] = dv.astype(jnp.bfloat16)

    @pl.when(step == 0)
    def _():
        first_ref[...] = head_ref[...]

    @pl.when(step == pl.num_programs(0) - 1)
    def _():
        column_ref[...] = jnp.sum(sum_ref[...], axis=0, keepdims=True)


def first_kernel(scalars, q_ref, sum_ref, first_ref, later_ref, dq_in, dk_in, *refs):
    count = len(refs) - 2
    keys = refs[:count]
    dq_ref, dk_ref = refs[count:]
    rows = q_ref.shape[0]
    cols = rows * count
    row, col, length = dims_of(scalars, rows, cols)
    query = half(q_ref[...], 0)
    scores = jnp.concatenate([rowdot(query, key[...]) for key in keys], axis=1)
    mask = (row > col) & (col >= 1) & (row < length) & (col < length) & (scores > 0.0)
    later = exact_sums(triangle(rows, True), sum_ref[...]) + later_ref[...]
    extra = jnp.where(mask, later, 0.0) * (-select_strength / cols)
    dscores = (first_ref[...] + extra).astype(jnp.bfloat16)
    acc = plain(dscores[:, 0:rows], keys[0][...])
    for b in range(1, count):
        acc = acc + plain(dscores[:, b * rows : (b + 1) * rows], keys[b][...])
    dq_ref[...] = dq_in[...] + half(acc * 0.125, 0).astype(jnp.bfloat16)
    scaled = query * jnp.asarray(0.125, jnp.bfloat16)
    for b in range(count):
        dk = coldot(dscores[:, b * rows : (b + 1) * rows], scaled)
        dk_ref[b] = dk_in[b] + dk.astype(jnp.bfloat16)


PAIR = 128


def pick(scalars, query, keys):
    rows, width = query.shape
    cols = rows * len(keys)
    one = pl.BlockSpec((rows, PAIR), lambda h, s: (0, 0))
    return pl.pallas_call(
        pick_kernel,
        name="pick",
        out_shape=(
            jax.ShapeDtypeStruct((rows, cols), jnp.float32),
            jax.ShapeDtypeStruct((1, cols), jnp.float32),
        ),
        grid_spec=pltpu.PrefetchScalarGridSpec(
            num_scalar_prefetch=1,
            grid=(1,),
            in_specs=[one] * (1 + len(keys)),
            out_specs=(
                pl.BlockSpec((rows, cols), lambda h, s: (0, 0)),
                pl.BlockSpec((1, cols), lambda h, s: (0, 0)),
            ),
        ),
    )(scalars, query, *keys)


def mix(scalars, query, carried, before, keys, values):
    rows, width = query.shape
    cols = rows * len(keys)
    pair = pl.BlockSpec((rows, PAIR), lambda h, s: (0, h))
    second = pl.BlockSpec((rows, PAIR), lambda h, s: (0, width // PAIR + h))
    full = pl.BlockSpec((rows, cols), lambda h, s: (0, 0))
    line = pl.BlockSpec((1, cols), lambda h, s: (0, 0))
    return pl.pallas_call(
        mix_kernel,
        name="mix",
        out_shape=(
            jax.ShapeDtypeStruct((rows, width), jnp.bfloat16),
            jax.ShapeDtypeStruct((rows, width), jnp.float32),
        ),
        grid_spec=pltpu.PrefetchScalarGridSpec(
            num_scalar_prefetch=1,
            grid=(width // PAIR,),
            in_specs=[pair, full, line] + [pair] * len(keys) + [second] * len(keys),
            out_specs=(pair, pair),
            scratch_shapes=[
                pltpu.VMEM((rows, cols), jnp.float32),
                pltpu.VMEM((2, rows, cols), jnp.float32),
                pltpu.VMEM((2, rows, cols), jnp.bfloat16),
            ],
        ),
    )(scalars, query, carried, before, *keys, *values)


def back(scalars, query, grad_mixed, total, carried, before, keys, values):
    rows, width = query.shape
    count = len(keys)
    cols = rows * count
    pair = pl.BlockSpec((rows, PAIR), lambda h, s: (0, h))
    second = pl.BlockSpec((rows, PAIR), lambda h, s: (0, width // PAIR + h))
    full = pl.BlockSpec((rows, cols), lambda h, s: (0, 0))
    line = pl.BlockSpec((1, cols), lambda h, s: (0, 0))
    blocks = pl.BlockSpec((count, rows, PAIR), lambda h, s: (0, 0, h))
    return pl.pallas_call(
        back_kernel,
        name="back",
        out_shape=(
            jax.ShapeDtypeStruct((rows, width), jnp.bfloat16),
            jax.ShapeDtypeStruct((count, rows, width), jnp.bfloat16),
            jax.ShapeDtypeStruct((count, rows, width), jnp.bfloat16),
            jax.ShapeDtypeStruct((rows, cols), jnp.float32),
            jax.ShapeDtypeStruct((rows, cols), jnp.float32),
            jax.ShapeDtypeStruct((1, cols), jnp.float32),
        ),
        grid_spec=pltpu.PrefetchScalarGridSpec(
            num_scalar_prefetch=1,
            grid=(width // PAIR,),
            in_specs=[pair, pair, pair, full, line] + [pair] * count + [second] * count,
            out_specs=(pair, blocks, blocks, full, full, line),
            scratch_shapes=[
                pltpu.VMEM((rows, cols), jnp.float32),
                pltpu.VMEM((2, rows, cols), jnp.float32),
                pltpu.VMEM((2, rows, cols), jnp.float32),
                pltpu.VMEM((2, rows, cols), jnp.bfloat16),
                pltpu.VMEM((2, rows, cols), jnp.bfloat16),
                pltpu.VMEM((rows, cols), jnp.float32),
            ],
        ),
    )(scalars, query, grad_mixed, total, carried, before, *keys, *values)


def first(scalars, query, sums, first_logits, later, dq, dk, keys):
    rows, width = query.shape
    count = len(keys)
    cols = rows * count
    one = pl.BlockSpec((rows, PAIR), lambda h, s: (0, 0))
    full = pl.BlockSpec((rows, cols), lambda h, s: (0, 0))
    line = pl.BlockSpec((1, cols), lambda h, s: (0, 0))
    blocks = pl.BlockSpec((count, rows, PAIR), lambda h, s: (0, 0, 0))
    return pl.pallas_call(
        first_kernel,
        name="first",
        out_shape=(
            jax.ShapeDtypeStruct((rows, width), jnp.bfloat16),
            jax.ShapeDtypeStruct((count, rows, width), jnp.bfloat16),
        ),
        grid_spec=pltpu.PrefetchScalarGridSpec(
            num_scalar_prefetch=1,
            grid=(1,),
            in_specs=[one, full, full, line, one, blocks] + [one] * count,
            out_specs=(one, blocks),
        ),
        input_output_aliases={5: 0, 6: 1},
    )(scalars, query, sums, first_logits, later, dq, dk, *keys)


def spread(array, axis):
    size = lax.axis_size(axis)
    got = {0: array}
    for bit in reversed(bits_of(axis)):
        for b in list(got):
            got[b ^ bit] = flip(got[b], axis, bit)
    return [got[b] for b in range(size)]


def collect(blocks, axis, steps):
    for bit in steps:
        size = blocks.shape[0] // 2
        pairs = blocks.reshape((size, 2) + blocks.shape[1:])
        blocks = pairs[:, 0] + flip(pairs[:, 1], axis, bit)
    return blocks


def line_prefix(array, axis, reverse):
    size = array.shape[0]
    total = array
    before = jnp.zeros_like(array)
    for bit in bits_of(axis):
        other = flip(total, axis, bit)
        other = jnp.stack([other[b ^ bit] for b in range(size)])
        is_upper = upper(axis, bit)
        take = jnp.logical_not(is_upper) if reverse else is_upper
        before = before + jnp.where(take, other, 0.0)
        total = total + other
    return before, total


def local(
    inputs,
    lengths,
    gain_attend,
    shift_attend,
    weight_query,
    weight_key,
    weight_value,
    weight_output,
    gain_mixer,
    shift_mixer,
    weight_inner,
    bias_inner,
    weight_outer,
    bias_outer,
    cotangent,
):
    layers = gain_attend.shape[0]
    seq_dev, local_len, width = inputs.shape
    seq_count = lax.axis_size("seq")
    devices = lax.axis_size(("dp", "seq"))
    is_last = lax.axis_index("seq") == seq_count - 1
    place = lax.axis_index("seq")
    key_place = (place ^ jnp.arange(seq_count, dtype=jnp.int32))[:, None] * local_len + jnp.arange(
        local_len, dtype=jnp.int32
    )
    valid_keys = key_place < lengths[0]
    scalars = jnp.stack([place, lengths[0]]).astype(jnp.int32)
    both = ("dp", "seq")
    parts = weight_inner.shape[2] // width
    vectors = jnp.concatenate(
        [gain_attend, shift_attend, gain_mixer, shift_mixer, bias_outer, bias_inner], axis=1
    )
    per = width // devices
    lots = pack(weight_query, weight_key, weight_value, weight_output, weight_inner, weight_outer)
    whole = [lax.all_gather(lot, both, axis=0, tiled=True) for lot in lots]
    orders = step_orders()
    line = jnp.pad(vectors.reshape(1, -1), ((0, 7), (0, width - vectors.size)))
    first_lot = gather_blocks(
        jnp.concatenate([weight_query[0], line]), tuple(reversed(orders[1]))
    )
    pair_lot = gather_blocks(
        jnp.concatenate([weight_key[0], weight_value[0]], axis=1), tuple(reversed(orders[0]))
    )
    vector_rows = first_lot[:, per, : vectors.size]
    first_query = first_lot[:, :per].reshape(width, width)
    first_pair = pair_lot.reshape(width, 2 * width)
    vector_rows = vector_rows.reshape(devices, layers, -1)
    small = [
        vector_rows[:, :, k * per : (k + 1) * per].transpose(1, 0, 2).reshape(layers, width)
        for k in range(5)
    ]
    bias_rows = vector_rows[:, :, 5 * per :].transpose(1, 0, 2).reshape(layers, width, parts)
    small.append(bias_rows.transpose(0, 2, 1).reshape(layers, parts * width))
    def square_of(matrix, k):
        return matrix[:, k * width : (k + 1) * width]

    last = 1 + 2 * parts

    def square_at(layer, k):
        if k >= 3:
            return square_of(whole[layer], k - 3)
        if layer == 0:
            return first_query if k == 0 else square_of(first_pair, k - 1)
        return square_of(whole[layer - 1], last + k)

    def pair_at(layer):
        if layer == 0:
            return first_pair
        return whole[layer - 1][:, (last + 1) * width : (last + 3) * width]

    def inner_at(layer):
        return whole[layer][:, width : (1 + parts) * width]

    small, hidden = lax.optimization_barrier((small, inputs))
    hidden = hidden.astype(jnp.float32)
    share_sum = jnp.zeros((), jnp.float32)
    saved = []
    for layer_index in range(layers):
        forward_gain_a, forward_shift_a, forward_gain_m, forward_shift_m = (
            small[k][layer_index] for k in range(4)
        )
        forward_b_outer, forward_b_inner = (small[k][layer_index] for k in (4, 5))
        forward_w_query = square_at(layer_index, 0)
        forward_w_output = square_at(layer_index, 3)
        forward_w_inner = inner_at(layer_index)
        forward_normed = (
            layer_norm(
                hidden, forward_gain_a.astype(jnp.float32), forward_shift_a.astype(jnp.float32)
            )
            .astype(jnp.bfloat16)
            .reshape(-1, width)
        )
        forward_pair = jnp.dot(
            forward_normed, pair_at(layer_index), preferred_element_type=jnp.float32
        ).astype(jnp.bfloat16)
        forward_query = jnp.dot(
            forward_normed, forward_w_query, preferred_element_type=jnp.float32
        ).astype(jnp.bfloat16)
        all_keys = all_values = spread(forward_pair, "seq")
        carried, column = pick(scalars, forward_query, all_keys)
        before, totals = line_prefix(column.reshape(seq_count, local_len), "seq", False)
        before = before.reshape(1, -1)
        forward_mixed, log_total = mix(
            scalars, forward_query, carried, before, all_keys, all_values
        )
        forward_after = hidden + jnp.dot(
            forward_mixed, forward_w_output, preferred_element_type=jnp.float32
        ).reshape(hidden.shape)
        forward_normed_two = (
            layer_norm(
                forward_after,
                forward_gain_m.astype(jnp.float32),
                forward_shift_m.astype(jnp.float32),
            )
            .astype(jnp.bfloat16)
            .reshape(-1, width)
        )
        forward_inner = jnp.dot(
            forward_normed_two, forward_w_inner, preferred_element_type=jnp.float32
        ) + forward_b_inner.astype(jnp.float32)
        forward_active = jax.nn.gelu(forward_inner).astype(jnp.bfloat16)
        outer = forward_b_outer.astype(jnp.float32)
        for k in range(parts):
            outer = outer + jnp.dot(
                square_of(forward_active, k),
                square_at(layer_index, 4 + parts + k),
                preferred_element_type=jnp.float32,
            )
        result = forward_after + outer.reshape(hidden.shape)
        share = jnp.where(
            is_last,
            jnp.sum(jnp.where(valid_keys, jnp.minimum(totals / share_level, 1.0), 0.0)),
            0.0,
        )
        forward_kept = (
            hidden,
            forward_normed,
            forward_query,
            all_keys,
            all_values,
            carried,
            before,
            log_total,
            forward_mixed,
            forward_after,
            forward_normed_two,
            forward_inner,
            forward_active,
        )
        hidden = result
        share_sum = share_sum + share
        saved.append(forward_kept)
    cotangent, _ = lax.optimization_barrier((cotangent, saved[-1][8]))
    grad_hidden = cotangent
    wide_sums = []
    held = []
    vector_grads = [None] * layers
    for layer_index in reversed(range(layers)):
        gain_a, shift_a, gain_m, shift_m = (small[k][layer_index] for k in range(4))
        w_query, w_key, w_value, w_output = (square_at(layer_index, k) for k in range(4))
        w_inner = inner_at(layer_index)
        (
            backward_hidden,
            normed,
            backward_query,
            all_keys,
            all_values,
            carried,
            before,
            log_total,
            mixed,
            after,
            normed_two,
            inner,
            active,
        ) = saved[layer_index]
        grad_y = grad_hidden.astype(jnp.bfloat16).reshape(-1, width)
        grad_b_outer = jnp.sum(grad_y, axis=0, dtype=jnp.float32)
        grad_w_outer = [product(square_of(active, k), grad_y, "tf,td->fd") for k in range(parts)]
        grad_active = jnp.concatenate(
            [
                product(grad_y, square_at(layer_index, 4 + parts + k), "td,fd->tf")
                for k in range(parts)
            ],
            axis=1,
        )
        gelu_back = jax.vjp(jax.nn.gelu, inner)[1]
        grad_inner = gelu_back(grad_active)[0].astype(jnp.bfloat16)
        grad_b_inner = jnp.sum(grad_inner, axis=0, dtype=jnp.float32)
        grad_w_inner = product(normed_two, grad_inner, "td,tf->df")
        grad_normed_two = product(grad_inner, w_inner, "tf,df->td").reshape(after.shape)
        norm_back_two = jax.vjp(
            layer_norm, after, gain_m.astype(jnp.float32), shift_m.astype(jnp.float32)
        )[1]
        after_part, grad_gain_m, grad_shift_m = norm_back_two(grad_normed_two)
        grad_after = grad_hidden + after_part
        grad_attn = grad_after.astype(jnp.bfloat16).reshape(-1, width)
        wide = [piece.astype(jnp.bfloat16) for piece in [grad_w_inner] + grad_w_outer]
        wide = jnp.concatenate(held[:2] + wide, axis=1)
        wide, grad_attn = lax.optimization_barrier((wide, grad_attn))
        wide_sums.append(lax.psum_scatter(wide, both, scatter_dimension=0, tiled=True))
        grad_mixed = product(grad_attn, w_output, "td,cd->tc").astype(jnp.bfloat16)
        grad_query, key_part, value_part, sums, first_logits, column_back = back(
            scalars, backward_query, grad_mixed, log_total, carried, before, all_keys, all_values
        )
        steps = bits_of("seq")
        grad_w_output = product(mixed, grad_attn, "tc,td->cd").astype(jnp.bfloat16)
        value_part = collect(value_part, "seq", steps[:1])
        later, _ = line_prefix(column_back.reshape(seq_count, local_len), "seq", True)
        grad_vals = collect(value_part, "seq", steps[1:])[0]
        later, grad_vals = lax.optimization_barrier((later, grad_vals))
        grad_query, key_part = first(
            scalars,
            backward_query,
            sums,
            first_logits,
            later.reshape(1, -1),
            grad_query,
            key_part,
            all_keys,
        )
        grad_keys = collect(key_part, "seq", steps)[0]
        grad_w_query = product(normed, grad_query, "tc,td->cd").astype(jnp.bfloat16)
        grad_keys, grad_vals, grad_w_query, grad_w_output = lax.optimization_barrier(
            (grad_keys, grad_vals, grad_w_query, grad_w_output)
        )
        grad_w_key = product(normed, grad_keys, "tc,td->cd")
        grad_w_value = product(normed, grad_vals, "tc,td->cd")
        grad_normed = (
            product(grad_query, w_query, "td,cd->tc")
            + product(grad_keys, w_key, "td,cd->tc")
            + product(grad_vals, w_value, "td,cd->tc")
        )
        norm_back_one = jax.vjp(
            layer_norm, backward_hidden, gain_a.astype(jnp.float32), shift_a.astype(jnp.float32)
        )[1]
        hidden_part, grad_gain_a, grad_shift_a = norm_back_one(
            grad_normed.reshape(backward_hidden.shape)
        )
        grad_hidden = grad_after + hidden_part
        low = jnp.bfloat16
        squares = [
            piece.astype(low)
            for piece in (grad_w_query, grad_w_key, grad_w_value, grad_w_output)
        ]
        kept = held
        held = squares
        vector_grads[layer_index] = jnp.concatenate(
            [
                grad_gain_a,
                grad_shift_a,
                grad_gain_m,
                grad_shift_m,
                grad_b_outer,
                grad_b_inner,
            ]
        )
    count = jnp.where(is_last, jnp.sum(lengths).astype(jnp.float32), 0.0)
    flat = jnp.concatenate(
        vector_grads + [jnp.broadcast_to(share_sum, (128,)), jnp.broadcast_to(count, (128,))]
    )
    flat = sum_all(flat.reshape(-1, 128), ("seq", "dp")).reshape(-1)
    size = (5 + parts) * width
    selected = flat[layers * size] / (layers * flat[layers * size + 128])
    place_of = lax.axis_index("dp") * seq_count + place
    vec = flat[: layers * size].reshape(layers, size)
    bias_grads = vec[:, 5 * width :].reshape(layers, parts, width).transpose(0, 2, 1)
    vec = jnp.concatenate([vec[:, : 5 * width], bias_grads.reshape(layers, -1)], axis=1)

    def mine(first, length):
        return lax.dynamic_slice_in_dim(
            vec[:, first * width : first * width + length], place_of * (length // devices),
            length // devices, axis=1,
        )

    rows = width // devices

    one = reduce_blocks(jnp.stack([squares[3], kept[3]]), orders[0])
    two = reduce_blocks(jnp.stack([squares[2], kept[2]]), orders[1])
    three = reduce_blocks(jnp.stack(squares[:2]), orders[2])
    square_sums = finish(wide_sums[1], wide_sums[0], one, two, three, width, parts)
    return (
        hidden,
        grad_hidden,
        mine(0, width),
        mine(1, width),
        square_sums[0],
        square_sums[1],
        square_sums[2],
        square_sums[3],
        mine(2, width),
        mine(3, width),
        square_sums[4],
        mine(5, parts * width),
        square_sums[5],
        mine(4, width),
        selected,
    )


def solution(mesh):
    placed = (
        P("dp", "seq", None),
        P("dp"),
        P(None, ("dp", "seq")),
        P(None, ("dp", "seq")),
        P(None, ("dp", "seq"), None),
        P(None, ("dp", "seq"), None),
        P(None, ("dp", "seq"), None),
        P(None, ("dp", "seq"), None),
        P(None, ("dp", "seq")),
        P(None, ("dp", "seq")),
        P(None, ("dp", "seq"), None),
        P(None, ("dp", "seq")),
        P(None, ("dp", "seq"), None),
        P(None, ("dp", "seq")),
        P("dp", "seq", None),
    )
    return jax.shard_map(
        local,
        mesh=mesh,
        in_specs=placed,
        out_specs=(
            P("dp", "seq", None),
            P("dp", "seq", None),
            P(None, ("dp", "seq")),
            P(None, ("dp", "seq")),
            P(None, ("dp", "seq"), None),
            P(None, ("dp", "seq"), None),
            P(None, ("dp", "seq"), None),
            P(None, ("dp", "seq"), None),
            P(None, ("dp", "seq")),
            P(None, ("dp", "seq")),
            P(None, ("dp", "seq"), None),
            P(None, ("dp", "seq")),
            P(None, ("dp", "seq"), None),
            P(None, ("dp", "seq")),
            P(),
        ),
        check_vma=False,
    )
```

```python
import jax
import jax.numpy as jnp
from jax import lax
from jax.experimental import pallas as pl
from jax.experimental.pallas import tpu as pltpu
from jax.sharding import PartitionSpec as P

HEADS = 12


norm_eps = 1e-05
share_level = 0.5
select_strength = 2.0
masked_value = -1e30


def layer_norm(hidden, gain, shift):
    average = jnp.mean(hidden, axis=-1, keepdims=True)
    centered = hidden - average
    spread = jnp.mean(centered * centered, axis=-1, keepdims=True)
    return centered * lax.rsqrt(spread + norm_eps) * gain + shift


def product(left, right, form):
    return jnp.einsum(form, left, right, preferred_element_type=jnp.float32)


def flip(array, axis, bit):
    size = lax.axis_size(axis)
    return lax.ppermute(array, axis, [(i, i ^ bit) for i in range(size)])


def bits_of(axis):
    size = lax.axis_size(axis)
    return [1 << k for k in range(size.bit_length() - 1)]


def upper(axis, bit):
    return (lax.axis_index(axis) & bit) != 0


share_unit = 8192.0


def digits_of(number, length):
    places = 2 * jnp.arange(length, dtype=jnp.int32)
    return ((number >> places) & 3).astype(jnp.float32)


def number_of(digits):
    return jnp.sum(digits * 4.0 ** jnp.arange(digits.shape[0], dtype=jnp.float32))


def split_rows(planes):
    count, rows, width = planes.shape
    dims = [("dp", bit) for bit in reversed(bits_of("dp"))]
    dims += [("seq", bit) for bit in reversed(bits_of("seq"))]
    blocks = planes.reshape((count,) + (2,) * len(dims) + (rows >> len(dims), width))
    return blocks, dims


def halve(blocks, dims, steps):
    dims = list(dims)
    for step in steps:
        axis, bit = step
        dim = 1 + dims.index(step)
        mine = upper(axis, bit).astype(jnp.int32)
        keep = lax.dynamic_index_in_dim(blocks, mine, dim, False)
        send = lax.dynamic_index_in_dim(blocks, 1 - mine, dim, False)
        blocks = keep + flip(send, axis, bit)
        dims.remove(step)
    return blocks, dims


def step_orders():
    near = [("seq", bit) for bit in bits_of("seq")][:1]
    across = [("seq", bit) for bit in bits_of("seq")][1:]
    beside = [("dp", bit) for bit in bits_of("dp")][:1]
    along = [("dp", bit) for bit in bits_of("dp")][1:]
    return (
        near + along + beside + across,
        near + beside + across + along,
        near + across + beside + along,
    )


def gather_blocks(array, steps):
    dims = []
    blocks = array
    for axis, bit in steps:
        other = flip(blocks, axis, bit)
        is_upper = upper(axis, bit)
        low = jnp.where(is_upper, other, blocks)
        high = jnp.where(is_upper, blocks, other)
        blocks = jnp.stack([low, high])
        dims.insert(0, (axis, bit))
    want = [("dp", bit) for bit in reversed(bits_of("dp"))]
    want += [("seq", bit) for bit in reversed(bits_of("seq"))]
    order = [dims.index(step) for step in want]
    blocks = blocks.transpose(order + [len(order), len(order) + 1])
    return blocks.reshape((-1,) + array.shape)


def one_hot(shape, hit):
    first = lax.broadcasted_iota(jnp.int32, shape, 0)
    second = lax.broadcasted_iota(jnp.int32, shape, 1)
    return jnp.where(hit(first, second), 1.0, 0.0).astype(jnp.bfloat16)


def pack_kernel(*refs):
    w_key, w_value, w_output, w_inner, w_outer = refs[:5]
    outs = refs[5:]
    layers, rows, width = w_key.shape
    parts = w_inner.shape[2] // width
    lane = width // 6
    span = lane * parts
    order = one_hot((span, span), lambda a, b: a == parts * (b % lane) + b // lane)
    for k in range(layers):
        out = outs[k]
        at = 0
        if k > 0:
            out[:, :width] = w_output[k]
            at = width
        for w in range(6):
            moved = plain(w_inner[k, :, w * span : (w + 1) * span], order).astype(jnp.bfloat16)
            for c in range(parts):
                start = at + c * width + w * lane
                out[:, start : start + lane] = moved[:, c * lane : (c + 1) * lane]
        at = at + parts * width
        for c in range(parts):
            take = one_hot((rows, parts * rows), lambda a, b, c=c: b == parts * a + c)
            out[:, at : at + width] = plain(take, w_outer[k]).astype(jnp.bfloat16)
            at = at + width
        if k + 1 < layers:
            for square in (w_key, w_value):
                out[:, at : at + width] = square[k + 1]
                at = at + width


def pack(*weights):
    layers, rows, width = weights[0].shape
    parts = weights[3].shape[2] // width
    return pl.pallas_call(
        pack_kernel,
        name="pack",
        out_shape=tuple(
            jax.ShapeDtypeStruct(
                (rows, (2 * parts + min(k, 1) + (2 if k + 1 < layers else 0)) * width),
                jnp.bfloat16,
            )
            for k in range(layers)
        ),
    )(*weights)


def spread_inner(grads, out, parts):
    lane = grads.shape[1] // (6 * parts)
    span = lane * parts
    order = one_hot((span, span), lambda a, b: b == parts * (a % lane) + a // lane)
    for w in range(6):
        pieces = [grads[:, (c * 6 + w) * lane : (c * 6 + w + 1) * lane] for c in range(parts)]
        out[:, w * span : (w + 1) * span] = plain(jnp.concatenate(pieces, axis=1), order)


def finish_kernel(late_ref, early_ref, one_ref, two_ref, three_ref, *outs):
    g_query, g_key, g_value, g_output, g_inner, g_outer = outs
    rows = late_ref.shape[0]
    width = g_query.shape[2]
    parts = g_inner.shape[2] // width
    g_query[0] = three_ref[0].astype(jnp.float32)
    g_key[0] = three_ref[1].astype(jnp.float32)
    g_value[0] = two_ref[0].astype(jnp.float32)
    g_output[0] = one_ref[0].astype(jnp.float32)
    g_query[1] = late_ref[:, :width].astype(jnp.float32)
    g_key[1] = late_ref[:, width : 2 * width].astype(jnp.float32)
    g_value[1] = two_ref[1].astype(jnp.float32)
    g_output[1] = one_ref[1].astype(jnp.float32)
    for k, ref, at in ((0, late_ref, 2 * width), (1, early_ref, 0)):
        spread_inner(ref[:, at : at + parts * width], g_inner.at[k], parts)
        at = at + parts * width
        total = 0.0
        for c in range(parts):
            put = one_hot((parts * rows, rows), lambda a, b, c=c: a == parts * b + c)
            total = total + plain(put, ref[:, at + c * width : at + (c + 1) * width])
        g_outer[k] = total


def finish(late, early, one, two, three, width, parts):
    rows = late.shape[0]
    square = jax.ShapeDtypeStruct((2, rows, width), jnp.float32)
    return pl.pallas_call(
        finish_kernel,
        name="finish",
        out_shape=(square,) * 4
        + (
            jax.ShapeDtypeStruct((2, rows, parts * width), jnp.float32),
            jax.ShapeDtypeStruct((2, parts * rows, width), jnp.float32),
        ),
    )(late, early, one, two, three)


def dims_of(scalars, rows, cols):
    place = scalars[0]
    length = scalars[1]
    local = rows
    count = cols // rows
    row = place * local + lax.broadcasted_iota(jnp.int32, (rows, cols), 0)
    within = lax.broadcasted_iota(jnp.int32, (1, local), 1)
    col = jnp.concatenate([(place ^ b) * local + within for b in range(count)], axis=1)
    return row, col, length


def half(array, which):
    lane = lax.broadcasted_iota(jnp.int32, array.shape, 1)
    keep = lane < array.shape[1] // 2
    if which:
        keep = jnp.logical_not(keep)
    return jnp.where(keep, array, jnp.zeros_like(array))


def rowdot(left, right):
    return lax.dot_general(
        left, right, (((1,), (1,)), ((), ())), preferred_element_type=jnp.float32
    )


def coldot(left, right):
    return lax.dot_general(
        left, right, (((0,), (0,)), ((), ())), preferred_element_type=jnp.float32
    )


def plain(left, right):
    return jnp.dot(left, right, preferred_element_type=jnp.float32)


def triangle(rows, upper):
    first = lax.broadcasted_iota(jnp.int32, (rows, rows), 0)
    second = lax.broadcasted_iota(jnp.int32, (rows, rows), 1)
    inside = (first < second) if upper else (first > second)
    return jnp.where(inside, 1.0, 0.0).astype(jnp.bfloat16)


def exact_sums(matrix, array):
    high = array.astype(jnp.bfloat16)
    rest = array - high.astype(jnp.float32)
    mid = rest.astype(jnp.bfloat16)
    low = (rest - mid.astype(jnp.float32)).astype(jnp.bfloat16)
    return plain(matrix, high) + plain(matrix, mid) + plain(matrix, low)


def pick_kernel(scalars, q_ref, *refs):
    count = len(refs) - 2
    keys = refs[:count]
    carried_ref, column_ref = refs[count:]
    rows = q_ref.shape[0]
    cols = rows * count
    row, col, length = dims_of(scalars, rows, cols)
    query = half(q_ref[...], 0)
    scores = jnp.concatenate([rowdot(query, key[...]) for key in keys], axis=1)
    mask = (row > col) & (col >= 1) & (row < length) & (col < length)
    select = jnp.where(mask, jnp.maximum(scores, 0.0), 0.0) * (0.125 * select_strength / cols)
    carried_ref[...] = exact_sums(triangle(rows, False), select)
    column_ref[...] = jnp.sum(select, axis=0, keepdims=True)


def fill_bias(scalars, bias_ref, carried_ref, before_ref):
    rows, cols = bias_ref.shape
    row, col, length = dims_of(scalars, rows, cols)
    carried = carried_ref[...] + before_ref[...]
    bias_ref[...] = jnp.where((row >= col) & (col < length), -carried, masked_value)


CHUNK = 32


def mix_kernel(scalars, q_ref, carried_ref, before_ref, *refs):
    count = (len(refs) - 5) // 2
    keys = refs[:count]
    values = refs[count : 2 * count]
    mixed_ref, total_ref, bias_ref, score_ref, prob_ref = refs[2 * count :]
    rows = q_ref.shape[0]

    @pl.when(pl.program_id(0) == 0)
    def _():
        fill_bias(scalars, bias_ref, carried_ref, before_ref)

    outs = []
    for which in range(2):
        query = half(q_ref[...], which) * jnp.asarray(0.125, jnp.bfloat16)
        for b in range(count):
            score_ref[which, :, b * rows : (b + 1) * rows] = rowdot(query, keys[b][...])
    for which in range(2):
        for chunk in range(rows // CHUNK):
            at = slice(chunk * CHUNK, (chunk + 1) * CHUNK)
            logits = score_ref[which, at, :] + bias_ref[at, :]
            peak = jnp.max(logits, axis=1, keepdims=True)
            expo = jnp.exp(logits - peak)
            denominator = jnp.sum(expo, axis=1, keepdims=True)
            prob_ref[which, at, :] = (expo * (1.0 / denominator)).astype(jnp.bfloat16)
            total = peak + jnp.log(denominator)
            width = total_ref.shape[1] // 2
            total_ref[at, which * width : (which + 1) * width] = jnp.broadcast_to(
                total, (CHUNK, width)
            )
        acc = plain(prob_ref[which, :, 0:rows], values[0][...])
        for b in range(1, count):
            acc = acc + plain(prob_ref[which, :, b * rows : (b + 1) * rows], values[b][...])
        outs.append(acc)
    mixed_ref[...] = (half(outs[0], 0) + half(outs[1], 1)).astype(jnp.bfloat16)


def back_kernel(scalars, q_ref, dm_ref, total_ref, carried_ref, before_ref, *refs):
    count = (len(refs) - 12) // 2
    keys = refs[:count]
    values = refs[count : 2 * count]
    (
        dq_ref,
        dk_ref,
        dv_ref,
        sum_ref,
        first_ref,
        column_ref,
        bias_ref,
        score_ref,
        dprob_ref,
        prob_ref,
        ds_ref,
        head_ref,
    ) = refs[2 * count :]
    rows = q_ref.shape[0]
    step = pl.program_id(0)

    @pl.when(step == 0)
    def _():
        fill_bias(scalars, bias_ref, carried_ref, before_ref)
        sum_ref[...] = jnp.zeros_like(sum_ref)

    later_heads = jnp.where(step == 0, 0.0, 1.0)
    eighth = jnp.asarray(0.125, jnp.bfloat16)
    queries = [half(q_ref[...], which) * eighth for which in range(2)]
    grads = [half(dm_ref[...], which) for which in range(2)]
    for which in range(2):
        for b in range(count):
            at = slice(b * rows, (b + 1) * rows)
            score_ref[which, :, at] = rowdot(queries[which], keys[b][...])
            dprob_ref[which, :, at] = rowdot(grads[which], values[b][...])
    for which in range(2):
        width = total_ref.shape[1] // 2
        for chunk in range(rows // CHUNK):
            at = slice(chunk * CHUNK, (chunk + 1) * CHUNK)
            total = total_ref[at, which * width : which * width + 1]
            probs = jnp.exp(score_ref[which, at, :] + bias_ref[at, :] - total)
            dprob = dprob_ref[which, at, :]
            delta = jnp.sum(probs * dprob, axis=1, keepdims=True)
            dlogits = probs * (dprob - delta)
            prob_ref[which, at, :] = probs.astype(jnp.bfloat16)
            sum_ref[at, :] = sum_ref[at, :] + dlogits
            if which == 0:
                head_ref[at, :] = dlogits
                dlogits = dlogits * later_heads
            ds_ref[which, at, :] = dlogits.astype(jnp.bfloat16)

    dq = []
    for which in range(2):
        acc = plain(ds_ref[which, :, 0:rows], keys[0][...])
        for b in range(1, count):
            acc = acc + plain(ds_ref[which, :, b * rows : (b + 1) * rows], keys[b][...])
        dq.append(acc)
    dq_ref[...] = ((half(dq[0], 0) + half(dq[1], 1)) * 0.125).astype(jnp.bfloat16)
    for b in range(count):
        at = slice(b * rows, (b + 1) * rows)
        dk = coldot(ds_ref[0, :, at], queries[0]) + coldot(ds_ref[1, :, at], queries[1])
        dv = coldot(prob_ref[0, :, at], grads[0]) + coldot(prob_ref[1, :, at], grads[1])
        dk_ref[b] = dk.astype(jnp.bfloat16)
        dv_ref[b] = dv.astype(jnp.bfloat16)

    @pl.when(step == 0)
    def _():
        first_ref[...] = head_ref[...]

    @pl.when(step == pl.num_programs(0) - 1)
    def _():
        column_ref[...] = jnp.sum(sum_ref[...], axis=0, keepdims=True)


def first_kernel(scalars, q_ref, sum_ref, first_ref, later_ref, dq_in, dk_in, *refs):
    count = len(refs) - 2
    keys = refs[:count]
    dq_ref, dk_ref = refs[count:]
    rows = q_ref.shape[0]
    cols = rows * count
    row, col, length = dims_of(scalars, rows, cols)
    query = half(q_ref[...], 0)
    scores = jnp.concatenate([rowdot(query, key[...]) for key in keys], axis=1)
    mask = (row > col) & (col >= 1) & (row < length) & (col < length) & (scores > 0.0)
    later = exact_sums(triangle(rows, True), sum_ref[...]) + later_ref[...]
    extra = jnp.where(mask, later, 0.0) * (-select_strength / cols)
    dscores = (first_ref[...] + extra).astype(jnp.bfloat16)
    acc = plain(dscores[:, 0:rows], keys[0][...])
    for b in range(1, count):
        acc = acc + plain(dscores[:, b * rows : (b + 1) * rows], keys[b][...])
    dq_ref[...] = dq_in[...] + half(acc * 0.125, 0).astype(jnp.bfloat16)
    scaled = query * jnp.asarray(0.125, jnp.bfloat16)
    for b in range(count):
        dk = coldot(dscores[:, b * rows : (b + 1) * rows], scaled)
        dk_ref[b] = dk_in[b] + dk.astype(jnp.bfloat16)


PAIR = 128


def pick(scalars, query, keys):
    rows, width = query.shape
    cols = rows * len(keys)
    one = pl.BlockSpec((rows, PAIR), lambda h, s: (0, 0))
    return pl.pallas_call(
        pick_kernel,
        name="pick",
        out_shape=(
            jax.ShapeDtypeStruct((rows, cols), jnp.float32),
            jax.ShapeDtypeStruct((1, cols), jnp.float32),
        ),
        grid_spec=pltpu.PrefetchScalarGridSpec(
            num_scalar_prefetch=1,
            grid=(1,),
            in_specs=[one] * (1 + len(keys)),
            out_specs=(
                pl.BlockSpec((rows, cols), lambda h, s: (0, 0)),
                pl.BlockSpec((1, cols), lambda h, s: (0, 0)),
            ),
        ),
    )(scalars, query, *keys)


def mix(scalars, query, carried, before, keys, values):
    rows, width = query.shape
    cols = rows * len(keys)
    pair = pl.BlockSpec((rows, PAIR), lambda h, s: (0, h))
    second = pl.BlockSpec((rows, PAIR), lambda h, s: (0, width // PAIR + h))
    full = pl.BlockSpec((rows, cols), lambda h, s: (0, 0))
    line = pl.BlockSpec((1, cols), lambda h, s: (0, 0))
    return pl.pallas_call(
        mix_kernel,
        name="mix",
        out_shape=(
            jax.ShapeDtypeStruct((rows, width), jnp.bfloat16),
            jax.ShapeDtypeStruct((rows, width), jnp.float32),
        ),
        grid_spec=pltpu.PrefetchScalarGridSpec(
            num_scalar_prefetch=1,
            grid=(width // PAIR,),
            in_specs=[pair, full, line] + [pair] * len(keys) + [second] * len(keys),
            out_specs=(pair, pair),
            scratch_shapes=[
                pltpu.VMEM((rows, cols), jnp.float32),
                pltpu.VMEM((2, rows, cols), jnp.float32),
                pltpu.VMEM((2, rows, cols), jnp.bfloat16),
            ],
        ),
    )(scalars, query, carried, before, *keys, *values)


def back(scalars, query, grad_mixed, total, carried, before, keys, values):
    rows, width = query.shape
    count = len(keys)
    cols = rows * count
    pair = pl.BlockSpec((rows, PAIR), lambda h, s: (0, h))
    second = pl.BlockSpec((rows, PAIR), lambda h, s: (0, width // PAIR + h))
    full = pl.BlockSpec((rows, cols), lambda h, s: (0, 0))
    line = pl.BlockSpec((1, cols), lambda h, s: (0, 0))
    blocks = pl.BlockSpec((count, rows, PAIR), lambda h, s: (0, 0, h))
    return pl.pallas_call(
        back_kernel,
        name="back",
        out_shape=(
            jax.ShapeDtypeStruct((rows, width), jnp.bfloat16),
            jax.ShapeDtypeStruct((count, rows, width), jnp.bfloat16),
            jax.ShapeDtypeStruct((count, rows, width), jnp.bfloat16),
            jax.ShapeDtypeStruct((rows, cols), jnp.float32),
            jax.ShapeDtypeStruct((rows, cols), jnp.float32),
            jax.ShapeDtypeStruct((1, cols), jnp.float32),
        ),
        grid_spec=pltpu.PrefetchScalarGridSpec(
            num_scalar_prefetch=1,
            grid=(width // PAIR,),
            in_specs=[pair, pair, pair, full, line] + [pair] * count + [second] * count,
            out_specs=(pair, blocks, blocks, full, full, line),
            scratch_shapes=[
                pltpu.VMEM((rows, cols), jnp.float32),
                pltpu.VMEM((2, rows, cols), jnp.float32),
                pltpu.VMEM((2, rows, cols), jnp.float32),
                pltpu.VMEM((2, rows, cols), jnp.bfloat16),
                pltpu.VMEM((2, rows, cols), jnp.bfloat16),
                pltpu.VMEM((rows, cols), jnp.float32),
            ],
        ),
    )(scalars, query, grad_mixed, total, carried, before, *keys, *values)


def first(scalars, query, sums, first_logits, later, dq, dk, keys):
    rows, width = query.shape
    count = len(keys)
    cols = rows * count
    one = pl.BlockSpec((rows, PAIR), lambda h, s: (0, 0))
    full = pl.BlockSpec((rows, cols), lambda h, s: (0, 0))
    line = pl.BlockSpec((1, cols), lambda h, s: (0, 0))
    blocks = pl.BlockSpec((count, rows, PAIR), lambda h, s: (0, 0, 0))
    return pl.pallas_call(
        first_kernel,
        name="first",
        out_shape=(
            jax.ShapeDtypeStruct((rows, width), jnp.bfloat16),
            jax.ShapeDtypeStruct((count, rows, width), jnp.bfloat16),
        ),
        grid_spec=pltpu.PrefetchScalarGridSpec(
            num_scalar_prefetch=1,
            grid=(1,),
            in_specs=[one, full, full, line, one, blocks] + [one] * count,
            out_specs=(one, blocks),
        ),
        input_output_aliases={5: 0, 6: 1},
    )(scalars, query, sums, first_logits, later, dq, dk, *keys)


def spread(array, axis):
    size = lax.axis_size(axis)
    got = {0: array}
    for bit in reversed(bits_of(axis)):
        for b in list(got):
            got[b ^ bit] = flip(got[b], axis, bit)
    return [got[b] for b in range(size)]


def collect(blocks, axis, steps):
    for bit in steps:
        size = blocks.shape[0] // 2
        pairs = blocks.reshape((size, 2) + blocks.shape[1:])
        blocks = pairs[:, 0] + flip(pairs[:, 1], axis, bit)
    return blocks


def line_prefix(array, axis, reverse):
    size = array.shape[0]
    total = array
    before = jnp.zeros_like(array)
    for bit in bits_of(axis):
        other = flip(total, axis, bit)
        other = jnp.stack([other[b ^ bit] for b in range(size)])
        is_upper = upper(axis, bit)
        take = jnp.logical_not(is_upper) if reverse else is_upper
        before = before + jnp.where(take, other, 0.0)
        total = total + other
    return before, total


def local(
    inputs,
    lengths,
    gain_attend,
    shift_attend,
    weight_query,
    weight_key,
    weight_value,
    weight_output,
    gain_mixer,
    shift_mixer,
    weight_inner,
    bias_inner,
    weight_outer,
    bias_outer,
    cotangent,
):
    layers = gain_attend.shape[0]
    seq_dev, local_len, width = inputs.shape
    seq_count = lax.axis_size("seq")
    devices = lax.axis_size(("dp", "seq"))
    is_last = lax.axis_index("seq") == seq_count - 1
    place = lax.axis_index("seq")
    key_place = (place ^ jnp.arange(seq_count, dtype=jnp.int32))[:, None] * local_len + jnp.arange(
        local_len, dtype=jnp.int32
    )
    valid_keys = key_place < lengths[0]
    scalars = jnp.stack([place, lengths[0]]).astype(jnp.int32)
    both = ("dp", "seq")
    parts = weight_inner.shape[2] // width
    vectors = jnp.concatenate(
        [gain_attend, shift_attend, gain_mixer, shift_mixer, bias_outer, bias_inner], axis=1
    )
    per = width // devices
    lots = pack(weight_key, weight_value, weight_output, weight_inner, weight_outer)
    whole = [lax.all_gather(lot, both, axis=0, tiled=True) for lot in lots]
    orders = step_orders()
    gather_orders = (tuple(reversed(orders[2])), tuple(reversed(orders[1])))
    line = jnp.pad(vectors.reshape(1, -1), ((0, 7), (0, width - vectors.size)))
    first_lot = gather_blocks(
        jnp.concatenate([weight_query[0], weight_output[0], line]), gather_orders[1]
    )
    pair_lot = gather_blocks(
        jnp.concatenate([weight_key[0], weight_value[0]] + list(weight_query[1:]), axis=1),
        gather_orders[0],
    )
    vector_rows = first_lot[:, 2 * per, : vectors.size]
    first_query = first_lot[:, :per].reshape(width, width)
    first_output = first_lot[:, per : 2 * per].reshape(width, width)
    first_pair = pair_lot.reshape(width, -1)
    vector_rows = vector_rows.reshape(devices, layers, -1)
    small = [
        vector_rows[:, :, k * per : (k + 1) * per].transpose(1, 0, 2).reshape(layers, width)
        for k in range(5)
    ]
    bias_rows = vector_rows[:, :, 5 * per :].transpose(1, 0, 2).reshape(layers, width, parts)
    small.append(bias_rows.transpose(0, 2, 1).reshape(layers, parts * width))
    def square_of(matrix, k):
        return matrix[:, k * width : (k + 1) * width]

    def square_at(layer, k):
        if layer == 0:
            if k == 0:
                return first_query
            if k < 3:
                return square_of(first_pair, k - 1)
            return first_output if k == 3 else square_of(whole[0], k - 4)
        if k == 0:
            return square_of(first_pair, 1 + layer)
        if k < 3:
            return square_of(whole[layer - 1], 2 * parts + min(layer - 1, 1) + k - 1)
        return square_of(whole[layer], k - 3)

    def pair_at(layer):
        if layer == 0:
            return first_pair[:, : 2 * width]
        at = (2 * parts + min(layer - 1, 1)) * width
        return whole[layer - 1][:, at : at + 2 * width]

    def inner_at(layer):
        at = min(layer, 1) * width
        return whole[layer][:, at : at + parts * width]

    small, hidden = lax.optimization_barrier((small, inputs))
    hidden = hidden.astype(jnp.float32)
    share_sum = jnp.zeros((), jnp.float32)
    saved = []
    for layer_index in range(layers):
        forward_gain_a, forward_shift_a, forward_gain_m, forward_shift_m = (
            small[k][layer_index] for k in range(4)
        )
        forward_b_outer, forward_b_inner = (small[k][layer_index] for k in (4, 5))
        forward_w_query = square_at(layer_index, 0)
        forward_w_output = square_at(layer_index, 3)
        forward_w_inner = inner_at(layer_index)
        forward_normed = (
            layer_norm(
                hidden, forward_gain_a.astype(jnp.float32), forward_shift_a.astype(jnp.float32)
            )
            .astype(jnp.bfloat16)
            .reshape(-1, width)
        )
        forward_pair = jnp.dot(
            forward_normed, pair_at(layer_index), preferred_element_type=jnp.float32
        ).astype(jnp.bfloat16)
        forward_query = jnp.dot(
            forward_normed, forward_w_query, preferred_element_type=jnp.float32
        ).astype(jnp.bfloat16)
        all_keys = all_values = spread(forward_pair, "seq")
        carried, column = pick(scalars, forward_query, all_keys)
        before, totals = line_prefix(column.reshape(seq_count, local_len), "seq", False)
        before = before.reshape(1, -1)
        forward_mixed, log_total = mix(
            scalars, forward_query, carried, before, all_keys, all_values
        )
        forward_after = hidden + jnp.dot(
            forward_mixed, forward_w_output, preferred_element_type=jnp.float32
        ).reshape(hidden.shape)
        forward_normed_two = (
            layer_norm(
                forward_after,
                forward_gain_m.astype(jnp.float32),
                forward_shift_m.astype(jnp.float32),
            )
            .astype(jnp.bfloat16)
            .reshape(-1, width)
        )
        forward_inner = jnp.dot(
            forward_normed_two, forward_w_inner, preferred_element_type=jnp.float32
        ) + forward_b_inner.astype(jnp.float32)
        forward_active = jax.nn.gelu(forward_inner).astype(jnp.bfloat16)
        outer = forward_b_outer.astype(jnp.float32)
        for k in range(parts):
            outer = outer + jnp.dot(
                square_of(forward_active, k),
                square_at(layer_index, 4 + parts + k),
                preferred_element_type=jnp.float32,
            )
        result = forward_after + outer.reshape(hidden.shape)
        share = jnp.where(
            is_last,
            jnp.sum(jnp.where(valid_keys, jnp.minimum(totals / share_level, 1.0), 0.0)),
            0.0,
        )
        forward_kept = (
            hidden,
            forward_normed,
            forward_query,
            all_keys,
            all_values,
            carried,
            before,
            log_total,
            forward_mixed,
            forward_after,
            forward_normed_two,
            forward_inner,
            forward_active,
        )
        hidden = result
        share_sum = share_sum + share
        saved.append(forward_kept)
    cotangent, _ = lax.optimization_barrier((cotangent, saved[-1][8]))
    grad_hidden = cotangent
    wide_sums = []
    held = []
    vector_grads = [None] * layers
    for layer_index in reversed(range(layers)):
        gain_a, shift_a, gain_m, shift_m = (small[k][layer_index] for k in range(4))
        w_query, w_key, w_value, w_output = (square_at(layer_index, k) for k in range(4))
        w_inner = inner_at(layer_index)
        (
            backward_hidden,
            normed,
            backward_query,
            all_keys,
            all_values,
            carried,
            before,
            log_total,
            mixed,
            after,
            normed_two,
            inner,
            active,
        ) = saved[layer_index]
        grad_y = grad_hidden.astype(jnp.bfloat16).reshape(-1, width)
        grad_b_outer = jnp.sum(grad_y, axis=0, dtype=jnp.float32)
        grad_w_outer = [product(square_of(active, k), grad_y, "tf,td->fd") for k in range(parts)]
        grad_active = jnp.concatenate(
            [
                product(grad_y, square_at(layer_index, 4 + parts + k), "td,fd->tf")
                for k in range(parts)
            ],
            axis=1,
        )
        gelu_back = jax.vjp(jax.nn.gelu, inner)[1]
        grad_inner = gelu_back(grad_active)[0].astype(jnp.bfloat16)
        grad_b_inner = jnp.sum(grad_inner, axis=0, dtype=jnp.float32)
        grad_w_inner = product(normed_two, grad_inner, "td,tf->df")
        wide = [piece.astype(jnp.bfloat16) for piece in [grad_w_inner] + grad_w_outer]
        wide = jnp.concatenate(held[:2] + wide, axis=1)
        grad_normed_two = product(grad_inner, w_inner, "tf,df->td").reshape(after.shape)
        norm_back_two = jax.vjp(
            layer_norm, after, gain_m.astype(jnp.float32), shift_m.astype(jnp.float32)
        )[1]
        after_part, grad_gain_m, grad_shift_m = norm_back_two(grad_normed_two)
        grad_after = grad_hidden + after_part
        grad_attn = grad_after.astype(jnp.bfloat16).reshape(-1, width)
        wide, grad_attn = lax.optimization_barrier((wide, grad_attn))
        wide_sums.append(lax.psum_scatter(wide, both, scatter_dimension=0, tiled=True))
        grad_mixed = product(grad_attn, w_output, "td,cd->tc").astype(jnp.bfloat16)
        grad_query, key_part, value_part, sums, first_logits, column_back = back(
            scalars, backward_query, grad_mixed, log_total, carried, before, all_keys, all_values
        )
        steps = bits_of("seq")
        grad_w_output = product(mixed, grad_attn, "tc,td->cd").astype(jnp.bfloat16)
        value_part = collect(value_part, "seq", steps[:1])
        later, _ = line_prefix(column_back.reshape(seq_count, local_len), "seq", True)
        grad_vals = collect(value_part, "seq", steps[1:])[0]
        later, grad_vals = lax.optimization_barrier((later, grad_vals))
        grad_query, key_part = first(
            scalars,
            backward_query,
            sums,
            first_logits,
            later.reshape(1, -1),
            grad_query,
            key_part,
            all_keys,
        )
        grad_keys = collect(key_part, "seq", steps)[0]
        grad_w_query = product(normed, grad_query, "tc,td->cd").astype(jnp.bfloat16)
        grad_keys, grad_vals, grad_w_query, grad_w_output = lax.optimization_barrier(
            (grad_keys, grad_vals, grad_w_query, grad_w_output)
        )
        grad_w_key = product(normed, grad_keys, "tc,td->cd")
        grad_w_value = product(normed, grad_vals, "tc,td->cd")
        grad_normed = (
            product(grad_query, w_query, "td,cd->tc")
            + product(grad_keys, w_key, "td,cd->tc")
            + product(grad_vals, w_value, "td,cd->tc")
        )
        norm_back_one = jax.vjp(
            layer_norm, backward_hidden, gain_a.astype(jnp.float32), shift_a.astype(jnp.float32)
        )[1]
        hidden_part, grad_gain_a, grad_shift_a = norm_back_one(
            grad_normed.reshape(backward_hidden.shape)
        )
        grad_hidden = grad_after + hidden_part
        low = jnp.bfloat16
        squares = [
            piece.astype(low)
            for piece in (grad_w_query, grad_w_key, grad_w_value, grad_w_output)
        ]
        kept = held
        held = squares
        vector_grads[layer_index] = jnp.concatenate(
            [
                grad_gain_a,
                grad_shift_a,
                grad_gain_m,
                grad_shift_m,
                grad_b_outer,
                grad_b_inner,
            ]
        )
    count = jnp.where(is_last, jnp.sum(lengths), 0)
    fixed = jnp.round(share_sum * share_unit).astype(jnp.int32)
    digits = jnp.concatenate([digits_of(fixed, 12), digits_of(count, 6)])
    vec = jnp.stack(vector_grads)
    bias_grads = vec[:, 5 * width :].reshape(layers, parts, width).transpose(0, 2, 1)
    vec = jnp.concatenate(
        [vec[:, : 5 * width].reshape(layers, 5, devices, per).transpose(2, 0, 1, 3).reshape(
            devices, layers, 5 * per
        ), bias_grads.reshape(layers, devices, parts * per).transpose(1, 0, 2)],
        axis=2,
    ).reshape(devices, 1, -1)
    vec = jnp.concatenate([vec, jnp.broadcast_to(digits, (devices, 1, 18))], axis=2)
    vec = jnp.pad(
        vec.astype(jnp.bfloat16), ((0, 0), (0, per - 1), (0, width - vec.shape[2]))
    ).reshape(width, width)
    lots = (
        [squares[3], kept[3]],
        [squares[2], kept[2]],
        [squares[0], squares[1], vec],
    )
    halves = []
    for lot, order in zip(lots, orders):
        blocks, dims = split_rows(jnp.stack(lot))
        halves.append(halve(blocks, dims, order[:2]))
    one, two, three = (
        halve(blocks, dims, order[2:])[0] for (blocks, dims), order in zip(halves, orders)
    )
    row = three[2, 0].astype(jnp.float32)
    size = layers * (5 + parts) * per
    mine_all = row[:size].reshape(layers, -1)
    share_all = number_of(row[size : size + 12]) / share_unit
    selected = share_all / (layers * number_of(row[size + 12 : size + 18]))

    def mine(first, length):
        return mine_all[:, first * per : first * per + length // devices]

    square_sums = finish(wide_sums[1], wide_sums[0], one, two, three, width, parts)
    return (
        hidden,
        grad_hidden,
        mine(0, width),
        mine(1, width),
        square_sums[0],
        square_sums[1],
        square_sums[2],
        square_sums[3],
        mine(2, width),
        mine(3, width),
        square_sums[4],
        mine(5, parts * width),
        square_sums[5],
        mine(4, width),
        selected,
    )


def solution(mesh):
    placed = (
        P("dp", "seq", None),
        P("dp"),
        P(None, ("dp", "seq")),
        P(None, ("dp", "seq")),
        P(None, ("dp", "seq"), None),
        P(None, ("dp", "seq"), None),
        P(None, ("dp", "seq"), None),
        P(None, ("dp", "seq"), None),
        P(None, ("dp", "seq")),
        P(None, ("dp", "seq")),
        P(None, ("dp", "seq"), None),
        P(None, ("dp", "seq")),
        P(None, ("dp", "seq"), None),
        P(None, ("dp", "seq")),
        P("dp", "seq", None),
    )
    return jax.shard_map(
        local,
        mesh=mesh,
        in_specs=placed,
        out_specs=(
            P("dp", "seq", None),
            P("dp", "seq", None),
            P(None, ("dp", "seq")),
            P(None, ("dp", "seq")),
            P(None, ("dp", "seq"), None),
            P(None, ("dp", "seq"), None),
            P(None, ("dp", "seq"), None),
            P(None, ("dp", "seq"), None),
            P(None, ("dp", "seq")),
            P(None, ("dp", "seq")),
            P(None, ("dp", "seq"), None),
            P(None, ("dp", "seq")),
            P(None, ("dp", "seq"), None),
            P(None, ("dp", "seq")),
            P(),
        ),
        check_vma=False,
    )
```

```python
import jax
import jax.numpy as jnp
from jax import lax
from jax.experimental import pallas as pl
from jax.experimental.pallas import tpu as pltpu
from jax.sharding import PartitionSpec as P

HEADS = 12


norm_eps = 1e-05
share_level = 0.5
select_strength = 2.0
masked_value = -1e30


def layer_norm(hidden, gain, shift):
    average = jnp.mean(hidden, axis=-1, keepdims=True)
    centered = hidden - average
    spread = jnp.mean(centered * centered, axis=-1, keepdims=True)
    return centered * lax.rsqrt(spread + norm_eps) * gain + shift


def product(left, right, form):
    return jnp.einsum(form, left, right, preferred_element_type=jnp.float32)


def flip(array, axis, bit):
    size = lax.axis_size(axis)
    return lax.ppermute(array, axis, [(i, i ^ bit) for i in range(size)])


def bits_of(axis):
    size = lax.axis_size(axis)
    return [1 << k for k in range(size.bit_length() - 1)]


def upper(axis, bit):
    return (lax.axis_index(axis) & bit) != 0


share_unit = 8192.0


def digits_of(number, length):
    places = 2 * jnp.arange(length, dtype=jnp.int32)
    return ((number >> places) & 3).astype(jnp.float32)


def number_of(digits):
    return jnp.sum(digits * 4.0 ** jnp.arange(digits.shape[0], dtype=jnp.float32))


def split_rows(planes):
    count, rows, width = planes.shape
    dims = [("dp", bit) for bit in reversed(bits_of("dp"))]
    dims += [("seq", bit) for bit in reversed(bits_of("seq"))]
    blocks = planes.reshape((count,) + (2,) * len(dims) + (rows >> len(dims), width))
    return blocks, dims


def halve(blocks, dims, steps):
    dims = list(dims)
    for step in steps:
        axis, bit = step
        dim = 1 + dims.index(step)
        mine = upper(axis, bit).astype(jnp.int32)
        keep = lax.dynamic_index_in_dim(blocks, mine, dim, False)
        send = lax.dynamic_index_in_dim(blocks, 1 - mine, dim, False)
        blocks = keep + flip(send, axis, bit)
        dims.remove(step)
    return blocks, dims


def step_orders():
    near = [("seq", bit) for bit in bits_of("seq")][:1]
    across = [("seq", bit) for bit in bits_of("seq")][1:]
    beside = [("dp", bit) for bit in bits_of("dp")][:1]
    along = [("dp", bit) for bit in bits_of("dp")][1:]
    return (
        near + along + beside + across,
        near + beside + across + along,
        near + across + beside + along,
    )


def gather_blocks(array, steps):
    dims = []
    blocks = array
    for axis, bit in steps:
        other = flip(blocks, axis, bit)
        is_upper = upper(axis, bit)
        low = jnp.where(is_upper, other, blocks)
        high = jnp.where(is_upper, blocks, other)
        blocks = jnp.stack([low, high])
        dims.insert(0, (axis, bit))
    want = [("dp", bit) for bit in reversed(bits_of("dp"))]
    want += [("seq", bit) for bit in reversed(bits_of("seq"))]
    order = [dims.index(step) for step in want]
    blocks = blocks.transpose(order + [len(order), len(order) + 1])
    return blocks.reshape((-1,) + array.shape)


def one_hot(shape, hit):
    first = lax.broadcasted_iota(jnp.int32, shape, 0)
    second = lax.broadcasted_iota(jnp.int32, shape, 1)
    return jnp.where(hit(first, second), 1.0, 0.0).astype(jnp.bfloat16)


def pack_kernel(*refs):
    w_key, w_value, w_output, w_inner, w_outer = refs[:5]
    outs = refs[5:]
    layers, rows, width = w_key.shape
    parts = w_inner.shape[2] // width
    lane = width // 6
    span = lane * parts
    order = one_hot((span, span), lambda a, b: a == parts * (b % lane) + b // lane)
    for k in range(layers):
        out = outs[k]
        at = 0
        if k > 0:
            out[:, :width] = w_output[k]
            at = width
        for w in range(6):
            moved = plain(w_inner[k, :, w * span : (w + 1) * span], order).astype(jnp.bfloat16)
            for c in range(parts):
                start = at + c * width + w * lane
                out[:, start : start + lane] = moved[:, c * lane : (c + 1) * lane]
        at = at + parts * width
        for c in range(parts):
            take = one_hot((rows, parts * rows), lambda a, b, c=c: b == parts * a + c)
            out[:, at : at + width] = plain(take, w_outer[k]).astype(jnp.bfloat16)
            at = at + width
        if k + 1 < layers:
            for square in (w_key, w_value):
                out[:, at : at + width] = square[k + 1]
                at = at + width


def pack(*weights):
    layers, rows, width = weights[0].shape
    parts = weights[3].shape[2] // width
    return pl.pallas_call(
        pack_kernel,
        name="pack",
        out_shape=tuple(
            jax.ShapeDtypeStruct(
                (rows, (2 * parts + min(k, 1) + (2 if k + 1 < layers else 0)) * width),
                jnp.bfloat16,
            )
            for k in range(layers)
        ),
    )(*weights)


def spread_inner(grads, out, parts):
    lane = grads.shape[1] // (6 * parts)
    span = lane * parts
    order = one_hot((span, span), lambda a, b: b == parts * (a % lane) + a // lane)
    for w in range(6):
        pieces = [grads[:, (c * 6 + w) * lane : (c * 6 + w + 1) * lane] for c in range(parts)]
        out[:, w * span : (w + 1) * span] = plain(jnp.concatenate(pieces, axis=1), order)


def finish_kernel(late_ref, early_ref, one_ref, two_ref, three_ref, *outs):
    g_query, g_key, g_value, g_output, g_inner, g_outer = outs
    rows = late_ref.shape[0]
    width = g_query.shape[2]
    parts = g_inner.shape[2] // width
    g_query[0] = three_ref[0].astype(jnp.float32)
    g_key[0] = three_ref[1].astype(jnp.float32)
    g_value[0] = two_ref[0].astype(jnp.float32)
    g_output[0] = one_ref[0].astype(jnp.float32)
    g_query[1] = late_ref[:, :width].astype(jnp.float32)
    g_key[1] = late_ref[:, width : 2 * width].astype(jnp.float32)
    g_value[1] = two_ref[1].astype(jnp.float32)
    g_output[1] = one_ref[1].astype(jnp.float32)
    for k, ref, at in ((0, late_ref, 2 * width), (1, early_ref, 0)):
        spread_inner(ref[:, at : at + parts * width], g_inner.at[k], parts)
        at = at + parts * width
        total = 0.0
        for c in range(parts):
            put = one_hot((parts * rows, rows), lambda a, b, c=c: a == parts * b + c)
            total = total + plain(put, ref[:, at + c * width : at + (c + 1) * width])
        g_outer[k] = total


def finish(late, early, one, two, three, width, parts):
    rows = late.shape[0]
    square = jax.ShapeDtypeStruct((2, rows, width), jnp.float32)
    return pl.pallas_call(
        finish_kernel,
        name="finish",
        out_shape=(square,) * 4
        + (
            jax.ShapeDtypeStruct((2, rows, parts * width), jnp.float32),
            jax.ShapeDtypeStruct((2, parts * rows, width), jnp.float32),
        ),
    )(late, early, one, two, three)


def dims_of(scalars, rows, cols):
    place = scalars[0]
    length = scalars[1]
    local = rows
    count = cols // rows
    row = place * local + lax.broadcasted_iota(jnp.int32, (rows, cols), 0)
    within = lax.broadcasted_iota(jnp.int32, (1, local), 1)
    col = jnp.concatenate([(place ^ b) * local + within for b in range(count)], axis=1)
    return row, col, length


def half(array, which):
    lane = lax.broadcasted_iota(jnp.int32, array.shape, 1)
    keep = lane < array.shape[1] // 2
    if which:
        keep = jnp.logical_not(keep)
    return jnp.where(keep, array, jnp.zeros_like(array))


def rowdot(left, right):
    return lax.dot_general(
        left, right, (((1,), (1,)), ((), ())), preferred_element_type=jnp.float32
    )


def coldot(left, right):
    return lax.dot_general(
        left, right, (((0,), (0,)), ((), ())), preferred_element_type=jnp.float32
    )


def plain(left, right):
    return jnp.dot(left, right, preferred_element_type=jnp.float32)


def triangle(rows, upper):
    first = lax.broadcasted_iota(jnp.int32, (rows, rows), 0)
    second = lax.broadcasted_iota(jnp.int32, (rows, rows), 1)
    inside = (first < second) if upper else (first > second)
    return jnp.where(inside, 1.0, 0.0).astype(jnp.bfloat16)


def exact_sums(matrix, array):
    high = array.astype(jnp.bfloat16)
    rest = array - high.astype(jnp.float32)
    mid = rest.astype(jnp.bfloat16)
    low = (rest - mid.astype(jnp.float32)).astype(jnp.bfloat16)
    return plain(matrix, high) + plain(matrix, mid) + plain(matrix, low)


def pick_kernel(scalars, q_ref, *refs):
    count = len(refs) - 2
    keys = refs[:count]
    carried_ref, column_ref = refs[count:]
    rows = q_ref.shape[0]
    cols = rows * count
    row, col, length = dims_of(scalars, rows, cols)
    query = half(q_ref[...], 0)
    scores = jnp.concatenate([rowdot(query, key[...]) for key in keys], axis=1)
    mask = (row > col) & (col >= 1) & (row < length) & (col < length)
    select = jnp.where(mask, jnp.maximum(scores, 0.0), 0.0) * (0.125 * select_strength / cols)
    carried_ref[...] = exact_sums(triangle(rows, False), select)
    column_ref[...] = jnp.sum(select, axis=0, keepdims=True)


def fill_bias(scalars, bias_ref, carried_ref, before_ref):
    rows, cols = bias_ref.shape
    row, col, length = dims_of(scalars, rows, cols)
    carried = carried_ref[...] + before_ref[...]
    bias_ref[...] = jnp.where((row >= col) & (col < length), -carried, masked_value)


CHUNK = 32


def mix_kernel(scalars, q_ref, carried_ref, before_ref, *refs):
    count = (len(refs) - 5) // 2
    keys = refs[:count]
    values = refs[count : 2 * count]
    mixed_ref, total_ref, bias_ref, score_ref, prob_ref = refs[2 * count :]
    rows = q_ref.shape[0]

    @pl.when(pl.program_id(0) == 0)
    def _():
        fill_bias(scalars, bias_ref, carried_ref, before_ref)

    outs = []
    for which in range(2):
        query = half(q_ref[...], which) * jnp.asarray(0.125, jnp.bfloat16)
        for b in range(count):
            score_ref[which, :, b * rows : (b + 1) * rows] = rowdot(query, keys[b][...])
    for which in range(2):
        for chunk in range(rows // CHUNK):
            at = slice(chunk * CHUNK, (chunk + 1) * CHUNK)
            logits = score_ref[which, at, :] + bias_ref[at, :]
            peak = jnp.max(logits, axis=1, keepdims=True)
            expo = jnp.exp(logits - peak)
            denominator = jnp.sum(expo, axis=1, keepdims=True)
            prob_ref[which, at, :] = (expo * (1.0 / denominator)).astype(jnp.bfloat16)
            total = peak + jnp.log(denominator)
            width = total_ref.shape[1] // 2
            total_ref[at, which * width : (which + 1) * width] = jnp.broadcast_to(
                total, (CHUNK, width)
            )
        acc = plain(prob_ref[which, :, 0:rows], values[0][...])
        for b in range(1, count):
            acc = acc + plain(prob_ref[which, :, b * rows : (b + 1) * rows], values[b][...])
        outs.append(acc)
    mixed_ref[...] = (half(outs[0], 0) + half(outs[1], 1)).astype(jnp.bfloat16)


def back_kernel(scalars, q_ref, dm_ref, total_ref, carried_ref, before_ref, *refs):
    count = (len(refs) - 12) // 2
    keys = refs[:count]
    values = refs[count : 2 * count]
    (
        dq_ref,
        dk_ref,
        dv_ref,
        sum_ref,
        first_ref,
        column_ref,
        bias_ref,
        score_ref,
        dprob_ref,
        prob_ref,
        ds_ref,
        head_ref,
    ) = refs[2 * count :]
    rows = q_ref.shape[0]
    step = pl.program_id(0)

    @pl.when(step == 0)
    def _():
        fill_bias(scalars, bias_ref, carried_ref, before_ref)
        sum_ref[...] = jnp.zeros_like(sum_ref)

    later_heads = jnp.where(step == 0, 0.0, 1.0)
    eighth = jnp.asarray(0.125, jnp.bfloat16)
    queries = [half(q_ref[...], which) * eighth for which in range(2)]
    grads = [half(dm_ref[...], which) for which in range(2)]
    for which in range(2):
        for b in range(count):
            at = slice(b * rows, (b + 1) * rows)
            score_ref[which, :, at] = rowdot(queries[which], keys[b][...])
            dprob_ref[which, :, at] = rowdot(grads[which], values[b][...])
    for which in range(2):
        width = total_ref.shape[1] // 2
        for chunk in range(rows // CHUNK):
            at = slice(chunk * CHUNK, (chunk + 1) * CHUNK)
            total = total_ref[at, which * width : which * width + 1]
            probs = jnp.exp(score_ref[which, at, :] + bias_ref[at, :] - total)
            dprob = dprob_ref[which, at, :]
            delta = jnp.sum(probs * dprob, axis=1, keepdims=True)
            dlogits = probs * (dprob - delta)
            prob_ref[which, at, :] = probs.astype(jnp.bfloat16)
            sum_ref[at, :] = sum_ref[at, :] + dlogits
            if which == 0:
                head_ref[at, :] = dlogits
                dlogits = dlogits * later_heads
            ds_ref[which, at, :] = dlogits.astype(jnp.bfloat16)

    dq = []
    for which in range(2):
        acc = plain(ds_ref[which, :, 0:rows], keys[0][...])
        for b in range(1, count):
            acc = acc + plain(ds_ref[which, :, b * rows : (b + 1) * rows], keys[b][...])
        dq.append(acc)
    dq_ref[...] = ((half(dq[0], 0) + half(dq[1], 1)) * 0.125).astype(jnp.bfloat16)
    for b in range(count):
        at = slice(b * rows, (b + 1) * rows)
        dk = coldot(ds_ref[0, :, at], queries[0]) + coldot(ds_ref[1, :, at], queries[1])
        dv = coldot(prob_ref[0, :, at], grads[0]) + coldot(prob_ref[1, :, at], grads[1])
        dk_ref[b] = dk.astype(jnp.bfloat16)
        dv_ref[b] = dv.astype(jnp.bfloat16)

    @pl.when(step == 0)
    def _():
        first_ref[...] = head_ref[...]

    @pl.when(step == pl.num_programs(0) - 1)
    def _():
        column_ref[...] = jnp.sum(sum_ref[...], axis=0, keepdims=True)


def first_kernel(scalars, q_ref, sum_ref, first_ref, later_ref, dq_in, dk_in, *refs):
    count = len(refs) - 2
    keys = refs[:count]
    dq_ref, dk_ref = refs[count:]
    rows = q_ref.shape[0]
    cols = rows * count
    row, col, length = dims_of(scalars, rows, cols)
    query = half(q_ref[...], 0)
    scores = jnp.concatenate([rowdot(query, key[...]) for key in keys], axis=1)
    mask = (row > col) & (col >= 1) & (row < length) & (col < length) & (scores > 0.0)
    later = exact_sums(triangle(rows, True), sum_ref[...]) + later_ref[...]
    extra = jnp.where(mask, later, 0.0) * (-select_strength / cols)
    dscores = (first_ref[...] + extra).astype(jnp.bfloat16)
    acc = plain(dscores[:, 0:rows], keys[0][...])
    for b in range(1, count):
        acc = acc + plain(dscores[:, b * rows : (b + 1) * rows], keys[b][...])
    dq_ref[...] = dq_in[...] + half(acc * 0.125, 0).astype(jnp.bfloat16)
    scaled = query * jnp.asarray(0.125, jnp.bfloat16)
    for b in range(count):
        dk = coldot(dscores[:, b * rows : (b + 1) * rows], scaled)
        dk_ref[b] = dk_in[b] + dk.astype(jnp.bfloat16)


PAIR = 128


def pick(scalars, query, keys):
    rows, width = query.shape
    cols = rows * len(keys)
    one = pl.BlockSpec((rows, PAIR), lambda h, s: (0, 0))
    return pl.pallas_call(
        pick_kernel,
        name="pick",
        out_shape=(
            jax.ShapeDtypeStruct((rows, cols), jnp.float32),
            jax.ShapeDtypeStruct((1, cols), jnp.float32),
        ),
        grid_spec=pltpu.PrefetchScalarGridSpec(
            num_scalar_prefetch=1,
            grid=(1,),
            in_specs=[one] * (1 + len(keys)),
            out_specs=(
                pl.BlockSpec((rows, cols), lambda h, s: (0, 0)),
                pl.BlockSpec((1, cols), lambda h, s: (0, 0)),
            ),
        ),
    )(scalars, query, *keys)


def mix(scalars, query, carried, before, keys, values):
    rows, width = query.shape
    cols = rows * len(keys)
    pair = pl.BlockSpec((rows, PAIR), lambda h, s: (0, h))
    second = pl.BlockSpec((rows, PAIR), lambda h, s: (0, width // PAIR + h))
    full = pl.BlockSpec((rows, cols), lambda h, s: (0, 0))
    line = pl.BlockSpec((1, cols), lambda h, s: (0, 0))
    return pl.pallas_call(
        mix_kernel,
        name="mix",
        out_shape=(
            jax.ShapeDtypeStruct((rows, width), jnp.bfloat16),
            jax.ShapeDtypeStruct((rows, width), jnp.float32),
        ),
        grid_spec=pltpu.PrefetchScalarGridSpec(
            num_scalar_prefetch=1,
            grid=(width // PAIR,),
            in_specs=[pair, full, line] + [pair] * len(keys) + [second] * len(keys),
            out_specs=(pair, pair),
            scratch_shapes=[
                pltpu.VMEM((rows, cols), jnp.float32),
                pltpu.VMEM((2, rows, cols), jnp.float32),
                pltpu.VMEM((2, rows, cols), jnp.bfloat16),
            ],
        ),
    )(scalars, query, carried, before, *keys, *values)


def back(scalars, query, grad_mixed, total, carried, before, keys, values):
    rows, width = query.shape
    count = len(keys)
    cols = rows * count
    pair = pl.BlockSpec((rows, PAIR), lambda h, s: (0, h))
    second = pl.BlockSpec((rows, PAIR), lambda h, s: (0, width // PAIR + h))
    full = pl.BlockSpec((rows, cols), lambda h, s: (0, 0))
    line = pl.BlockSpec((1, cols), lambda h, s: (0, 0))
    blocks = pl.BlockSpec((count, rows, PAIR), lambda h, s: (0, 0, h))
    return pl.pallas_call(
        back_kernel,
        name="back",
        out_shape=(
            jax.ShapeDtypeStruct((rows, width), jnp.bfloat16),
            jax.ShapeDtypeStruct((count, rows, width), jnp.bfloat16),
            jax.ShapeDtypeStruct((count, rows, width), jnp.bfloat16),
            jax.ShapeDtypeStruct((rows, cols), jnp.float32),
            jax.ShapeDtypeStruct((rows, cols), jnp.float32),
            jax.ShapeDtypeStruct((1, cols), jnp.float32),
        ),
        grid_spec=pltpu.PrefetchScalarGridSpec(
            num_scalar_prefetch=1,
            grid=(width // PAIR,),
            in_specs=[pair, pair, pair, full, line] + [pair] * count + [second] * count,
            out_specs=(pair, blocks, blocks, full, full, line),
            scratch_shapes=[
                pltpu.VMEM((rows, cols), jnp.float32),
                pltpu.VMEM((2, rows, cols), jnp.float32),
                pltpu.VMEM((2, rows, cols), jnp.float32),
                pltpu.VMEM((2, rows, cols), jnp.bfloat16),
                pltpu.VMEM((2, rows, cols), jnp.bfloat16),
                pltpu.VMEM((rows, cols), jnp.float32),
            ],
        ),
    )(scalars, query, grad_mixed, total, carried, before, *keys, *values)


def first(scalars, query, sums, first_logits, later, dq, dk, keys):
    rows, width = query.shape
    count = len(keys)
    cols = rows * count
    one = pl.BlockSpec((rows, PAIR), lambda h, s: (0, 0))
    full = pl.BlockSpec((rows, cols), lambda h, s: (0, 0))
    line = pl.BlockSpec((1, cols), lambda h, s: (0, 0))
    blocks = pl.BlockSpec((count, rows, PAIR), lambda h, s: (0, 0, 0))
    return pl.pallas_call(
        first_kernel,
        name="first",
        out_shape=(
            jax.ShapeDtypeStruct((rows, width), jnp.bfloat16),
            jax.ShapeDtypeStruct((count, rows, width), jnp.bfloat16),
        ),
        grid_spec=pltpu.PrefetchScalarGridSpec(
            num_scalar_prefetch=1,
            grid=(1,),
            in_specs=[one, full, full, line, one, blocks] + [one] * count,
            out_specs=(one, blocks),
        ),
        input_output_aliases={5: 0, 6: 1},
    )(scalars, query, sums, first_logits, later, dq, dk, *keys)


def spread(array, axis):
    size = lax.axis_size(axis)
    got = {0: array}
    for bit in reversed(bits_of(axis)):
        for b in list(got):
            got[b ^ bit] = flip(got[b], axis, bit)
    return [got[b] for b in range(size)]


def collect(blocks, axis, steps):
    for bit in steps:
        size = blocks.shape[0] // 2
        pairs = blocks.reshape((size, 2) + blocks.shape[1:])
        blocks = pairs[:, 0] + flip(pairs[:, 1], axis, bit)
    return blocks


def line_prefix(array, axis, reverse):
    size = array.shape[0]
    total = array
    before = jnp.zeros_like(array)
    for bit in bits_of(axis):
        other = flip(total, axis, bit)
        other = jnp.stack([other[b ^ bit] for b in range(size)])
        is_upper = upper(axis, bit)
        take = jnp.logical_not(is_upper) if reverse else is_upper
        before = before + jnp.where(take, other, 0.0)
        total = total + other
    return before, total


def local(
    inputs,
    lengths,
    gain_attend,
    shift_attend,
    weight_query,
    weight_key,
    weight_value,
    weight_output,
    gain_mixer,
    shift_mixer,
    weight_inner,
    bias_inner,
    weight_outer,
    bias_outer,
    cotangent,
):
    layers = gain_attend.shape[0]
    seq_dev, local_len, width = inputs.shape
    seq_count = lax.axis_size("seq")
    devices = lax.axis_size(("dp", "seq"))
    is_last = lax.axis_index("seq") == seq_count - 1
    place = lax.axis_index("seq")
    key_place = (place ^ jnp.arange(seq_count, dtype=jnp.int32))[:, None] * local_len + jnp.arange(
        local_len, dtype=jnp.int32
    )
    valid_keys = key_place < lengths[0]
    scalars = jnp.stack([place, lengths[0]]).astype(jnp.int32)
    both = ("dp", "seq")
    parts = weight_inner.shape[2] // width
    vectors = jnp.concatenate(
        [gain_attend, shift_attend, gain_mixer, shift_mixer, bias_outer, bias_inner], axis=1
    )
    per = width // devices
    lots = pack(weight_key, weight_value, weight_output, weight_inner, weight_outer)
    whole = [lax.all_gather(lot, both, axis=0, tiled=True) for lot in lots]
    orders = step_orders()
    gather_orders = (tuple(reversed(orders[2])), tuple(reversed(orders[1])))
    line = jnp.pad(vectors.reshape(1, -1), ((0, 7), (0, width - vectors.size)))
    first_lot = gather_blocks(
        jnp.concatenate([weight_query[0], weight_output[0], line]), gather_orders[1]
    )
    pair_lot = gather_blocks(
        jnp.concatenate([weight_key[0], weight_value[0]] + list(weight_query[1:]), axis=1),
        gather_orders[0],
    )
    vector_rows = first_lot[:, 2 * per, : vectors.size]
    first_query = first_lot[:, :per].reshape(width, width)
    first_output = first_lot[:, per : 2 * per].reshape(width, width)
    first_pair = pair_lot.reshape(width, -1)
    vector_rows = vector_rows.reshape(devices, layers, -1)
    small = [
        vector_rows[:, :, k * per : (k + 1) * per].transpose(1, 0, 2).reshape(layers, width)
        for k in range(5)
    ]
    bias_rows = vector_rows[:, :, 5 * per :].transpose(1, 0, 2).reshape(layers, width, parts)
    small.append(bias_rows.transpose(0, 2, 1).reshape(layers, parts * width))
    def square_of(matrix, k):
        return matrix[:, k * width : (k + 1) * width]

    def square_at(layer, k):
        if layer == 0:
            if k == 0:
                return first_query
            if k < 3:
                return square_of(first_pair, k - 1)
            return first_output if k == 3 else square_of(whole[0], k - 4)
        if k == 0:
            return square_of(first_pair, 1 + layer)
        if k < 3:
            return square_of(whole[layer - 1], 2 * parts + min(layer - 1, 1) + k - 1)
        return square_of(whole[layer], k - 3)

    def pair_at(layer):
        if layer == 0:
            return first_pair[:, : 2 * width]
        at = (2 * parts + min(layer - 1, 1)) * width
        return whole[layer - 1][:, at : at + 2 * width]

    def inner_at(layer):
        at = min(layer, 1) * width
        return whole[layer][:, at : at + parts * width]

    small, hidden = lax.optimization_barrier((small, inputs))
    hidden = hidden.astype(jnp.float32)
    share_sum = jnp.zeros((), jnp.float32)
    saved = []
    for layer_index in range(layers):
        forward_gain_a, forward_shift_a, forward_gain_m, forward_shift_m = (
            small[k][layer_index] for k in range(4)
        )
        forward_b_outer, forward_b_inner = (small[k][layer_index] for k in (4, 5))
        forward_w_query = square_at(layer_index, 0)
        forward_w_output = square_at(layer_index, 3)
        forward_w_inner = inner_at(layer_index)
        forward_normed = (
            layer_norm(
                hidden, forward_gain_a.astype(jnp.float32), forward_shift_a.astype(jnp.float32)
            )
            .astype(jnp.bfloat16)
            .reshape(-1, width)
        )
        forward_pair = jnp.dot(
            forward_normed, pair_at(layer_index), preferred_element_type=jnp.float32
        ).astype(jnp.bfloat16)
        forward_query = jnp.dot(
            forward_normed, forward_w_query, preferred_element_type=jnp.float32
        ).astype(jnp.bfloat16)
        all_keys = all_values = spread(forward_pair, "seq")
        carried, column = pick(scalars, forward_query, all_keys)
        before, totals = line_prefix(column.reshape(seq_count, local_len), "seq", False)
        before = before.reshape(1, -1)
        forward_mixed, log_total = mix(
            scalars, forward_query, carried, before, all_keys, all_values
        )
        forward_after = hidden + jnp.dot(
            forward_mixed, forward_w_output, preferred_element_type=jnp.float32
        ).reshape(hidden.shape)
        forward_normed_two = (
            layer_norm(
                forward_after,
                forward_gain_m.astype(jnp.float32),
                forward_shift_m.astype(jnp.float32),
            )
            .astype(jnp.bfloat16)
            .reshape(-1, width)
        )
        forward_inner = jnp.dot(
            forward_normed_two, forward_w_inner, preferred_element_type=jnp.float32
        ) + forward_b_inner.astype(jnp.float32)
        forward_active = jax.nn.gelu(forward_inner).astype(jnp.bfloat16)
        outer = forward_b_outer.astype(jnp.float32)
        for k in range(parts):
            outer = outer + jnp.dot(
                square_of(forward_active, k),
                square_at(layer_index, 4 + parts + k),
                preferred_element_type=jnp.float32,
            )
        result = forward_after + outer.reshape(hidden.shape)
        share = jnp.where(
            is_last,
            jnp.sum(jnp.where(valid_keys, jnp.minimum(totals / share_level, 1.0), 0.0)),
            0.0,
        )
        forward_kept = (
            hidden,
            forward_normed,
            forward_query,
            all_keys,
            all_values,
            carried,
            before,
            log_total,
            forward_mixed,
            forward_after,
            forward_normed_two,
            forward_inner,
            forward_active,
        )
        hidden = result
        share_sum = share_sum + share
        saved.append(forward_kept)
    cotangent, _ = lax.optimization_barrier((cotangent, saved[-1][8]))
    grad_hidden = cotangent
    wide_sums = []
    held = []
    vector_grads = [None] * layers
    for layer_index in reversed(range(layers)):
        gain_a, shift_a, gain_m, shift_m = (small[k][layer_index] for k in range(4))
        w_query, w_key, w_value, w_output = (square_at(layer_index, k) for k in range(4))
        w_inner = inner_at(layer_index)
        (
            backward_hidden,
            normed,
            backward_query,
            all_keys,
            all_values,
            carried,
            before,
            log_total,
            mixed,
            after,
            normed_two,
            inner,
            active,
        ) = saved[layer_index]
        grad_y = grad_hidden.astype(jnp.bfloat16).reshape(-1, width)
        grad_b_outer = jnp.sum(grad_y, axis=0, dtype=jnp.float32)
        grad_w_outer = [product(square_of(active, k), grad_y, "tf,td->fd") for k in range(parts)]
        grad_active = jnp.concatenate(
            [
                product(grad_y, square_at(layer_index, 4 + parts + k), "td,fd->tf")
                for k in range(parts)
            ],
            axis=1,
        )
        gelu_back = jax.vjp(jax.nn.gelu, inner)[1]
        grad_inner = gelu_back(grad_active)[0].astype(jnp.bfloat16)
        grad_b_inner = jnp.sum(grad_inner, axis=0, dtype=jnp.float32)
        grad_w_inner = product(normed_two, grad_inner, "td,tf->df")
        wide = [piece.astype(jnp.bfloat16) for piece in [grad_w_inner] + grad_w_outer]
        wide = jnp.concatenate(held[:2] + wide, axis=1)
        grad_normed_two = product(grad_inner, w_inner, "tf,df->td").reshape(after.shape)
        norm_back_two = jax.vjp(
            layer_norm, after, gain_m.astype(jnp.float32), shift_m.astype(jnp.float32)
        )[1]
        after_part, grad_gain_m, grad_shift_m = norm_back_two(grad_normed_two)
        grad_after = grad_hidden + after_part
        grad_attn = grad_after.astype(jnp.bfloat16).reshape(-1, width)
        wide, grad_attn = lax.optimization_barrier((wide, grad_attn))
        wide_sums.append(lax.psum_scatter(wide, both, scatter_dimension=0, tiled=True))
        grad_mixed = product(grad_attn, w_output, "td,cd->tc").astype(jnp.bfloat16)
        grad_query, key_part, value_part, sums, first_logits, column_back = back(
            scalars, backward_query, grad_mixed, log_total, carried, before, all_keys, all_values
        )
        steps = bits_of("seq")
        grad_w_output = product(mixed, grad_attn, "tc,td->cd").astype(jnp.bfloat16)
        value_part = collect(value_part, "seq", steps[:1])
        later, _ = line_prefix(column_back.reshape(seq_count, local_len), "seq", True)
        grad_vals = collect(value_part, "seq", steps[1:])[0]
        later, grad_vals = lax.optimization_barrier((later, grad_vals))
        grad_query, key_part = first(
            scalars,
            backward_query,
            sums,
            first_logits,
            later.reshape(1, -1),
            grad_query,
            key_part,
            all_keys,
        )
        grad_keys = collect(key_part, "seq", steps)[0]
        grad_w_query = product(normed, grad_query, "tc,td->cd").astype(jnp.bfloat16)
        grad_keys, grad_vals, grad_w_query, grad_w_output = lax.optimization_barrier(
            (grad_keys, grad_vals, grad_w_query, grad_w_output)
        )
        grad_w_key = product(normed, grad_keys, "tc,td->cd")
        grad_w_value = product(normed, grad_vals, "tc,td->cd")
        grad_normed = (
            product(grad_query, w_query, "td,cd->tc")
            + product(grad_keys, w_key, "td,cd->tc")
            + product(grad_vals, w_value, "td,cd->tc")
        )
        norm_back_one = jax.vjp(
            layer_norm, backward_hidden, gain_a.astype(jnp.float32), shift_a.astype(jnp.float32)
        )[1]
        hidden_part, grad_gain_a, grad_shift_a = norm_back_one(
            grad_normed.reshape(backward_hidden.shape)
        )
        grad_hidden = grad_after + hidden_part
        low = jnp.bfloat16
        squares = [
            piece.astype(low)
            for piece in (grad_w_query, grad_w_key, grad_w_value, grad_w_output)
        ]
        kept = held
        held = squares
        vector_grads[layer_index] = jnp.concatenate(
            [
                grad_gain_a,
                grad_shift_a,
                grad_gain_m,
                grad_shift_m,
                grad_b_outer,
                grad_b_inner,
            ]
        )
    count = jnp.where(is_last, jnp.sum(lengths), 0)
    fixed = jnp.round(share_sum * share_unit).astype(jnp.int32)
    digits = jnp.concatenate([digits_of(fixed, 12), digits_of(count, 6)])
    vec = jnp.stack(vector_grads)
    bias_grads = vec[:, 5 * width :].reshape(layers, parts, width).transpose(0, 2, 1)
    vec = jnp.concatenate(
        [vec[:, : 5 * width].reshape(layers, 5, devices, per).transpose(2, 0, 1, 3).reshape(
            devices, layers, 5 * per
        ), bias_grads.reshape(layers, devices, parts * per).transpose(1, 0, 2)],
        axis=2,
    ).reshape(devices, 1, -1)
    vec = jnp.concatenate([vec, jnp.broadcast_to(digits, (devices, 1, 18))], axis=2)
    vec = jnp.pad(vec.astype(jnp.bfloat16), ((0, 0), (0, 7), (0, width - vec.shape[2])))
    ends = [square.reshape(devices, per, width) for square in squares[:2]] + [vec]
    ends = jnp.concatenate(ends, axis=1).reshape(1, -1, width)
    lots = (
        jnp.stack([squares[3], kept[3]]),
        jnp.stack([squares[2], kept[2]]),
        ends,
    )
    halves = []
    halving = (orders[2], orders[0], orders[1])
    for lot, order in zip(lots, halving):
        blocks, dims = split_rows(lot)
        halves.append(halve(blocks, dims, order[:2]))
    one, two, three = (
        halve(blocks, dims, order[2:])[0] for (blocks, dims), order in zip(halves, halving)
    )
    row = three[0, 2 * per].astype(jnp.float32)
    three = three[0, : 2 * per].reshape(2, per, width)
    size = layers * (5 + parts) * per
    mine_all = row[:size].reshape(layers, -1)
    share_all = number_of(row[size : size + 12]) / share_unit
    selected = share_all / (layers * number_of(row[size + 12 : size + 18]))

    def mine(first, length):
        return mine_all[:, first * per : first * per + length // devices]

    square_sums = finish(wide_sums[1], wide_sums[0], one, two, three, width, parts)
    return (
        hidden,
        grad_hidden,
        mine(0, width),
        mine(1, width),
        square_sums[0],
        square_sums[1],
        square_sums[2],
        square_sums[3],
        mine(2, width),
        mine(3, width),
        square_sums[4],
        mine(5, parts * width),
        square_sums[5],
        mine(4, width),
        selected,
    )


def solution(mesh):
    placed = (
        P("dp", "seq", None),
        P("dp"),
        P(None, ("dp", "seq")),
        P(None, ("dp", "seq")),
        P(None, ("dp", "seq"), None),
        P(None, ("dp", "seq"), None),
        P(None, ("dp", "seq"), None),
        P(None, ("dp", "seq"), None),
        P(None, ("dp", "seq")),
        P(None, ("dp", "seq")),
        P(None, ("dp", "seq"), None),
        P(None, ("dp", "seq")),
        P(None, ("dp", "seq"), None),
        P(None, ("dp", "seq")),
        P("dp", "seq", None),
    )
    return jax.shard_map(
        local,
        mesh=mesh,
        in_specs=placed,
        out_specs=(
            P("dp", "seq", None),
            P("dp", "seq", None),
            P(None, ("dp", "seq")),
            P(None, ("dp", "seq")),
            P(None, ("dp", "seq"), None),
            P(None, ("dp", "seq"), None),
            P(None, ("dp", "seq"), None),
            P(None, ("dp", "seq"), None),
            P(None, ("dp", "seq")),
            P(None, ("dp", "seq")),
            P(None, ("dp", "seq"), None),
            P(None, ("dp", "seq")),
            P(None, ("dp", "seq"), None),
            P(None, ("dp", "seq")),
            P(),
        ),
        check_vma=False,
    )
```
